256 devices in a mesh: req: 32 (over z, x_hi, core), kvh: 4 (over y), exp: 2 (over x_lo).
Axes of the slice: x: 4 (x_hi: 2, x_lo: 2; x = x_hi * 2 + x_lo), y: 4, z: 8, core: 2. Of those that a mesh axis runs over, the one named last changes fastest.
Arguments:
- queries: bfloat16 [4096, 2048], P(('req', 'exp'), 'kvh'), may hold values from -170 to 170
- keys: bfloat16 [4096, 4, 64, 128], P(('req', 'exp'), 'kvh'), may hold values from -6 to 6
- values: bfloat16 [4096, 4, 64, 128], P(('req', 'exp'), 'kvh'), may hold values from -6 to 6
- lengths: int32 [4096], P('req'), may hold values from 2 to 64
- out_weight: bfloat16 [2048, 2048], P(('kvh', 'exp')), may hold values from -0.125 to 0.125
- residual: bfloat16 [4096, 2048], P('req'), may hold values from -54 to 54
- norm_gain: float32 [2048], replicated, may hold values from 0.5 to 2
- expert_ids: int32 [4096, 8], P('req'), may hold values from 0 to 63, as said below
- gate_weights: float32 [4096, 8], P('req'), may hold values from 0.2 to 1
- replica_map: int32 [128], replicated, may hold values from 0 to 63, as said below
- w_gate: bfloat16 [128, 2048, 384], P(('req', 'kvh'), None, 'exp')
- w_up: bfloat16 [128, 2048, 384], P(('req', 'kvh'), None, 'exp')
- w_down: bfloat16 [128, 384, 2048], P(('req', 'kvh'), 'exp')
Outputs:
- layer_out: bfloat16 [4096, 2048], P('req', ('kvh', 'exp'))
The draws below stay inside these ranges and needn't reach their ends.
Inputs may be any that keep to these rules, and one draw needn't show every extreme that they name: `replica_map`: every one of the 64 experts is served by one or more slots; slots that serve one expert hold equal weights in w_gate, w_up and w_down. `expert_ids`: A token names 8 different experts and every expert is named by some token; among the 128 tokens of one req index no expert is named by more than 24 tokens, and in every req index some expert is named by exactly 24.
All inputs are finite; a program needn't handle non-finite values.
Results may differ from the reference program's by a relative error of at most 0.008.
Values may be sent and summed in bfloat16 or wider, within the bound.
A program may use at most 64 MiB of HBM per device.

```python
import math
import jax
import jax.numpy as jnp
from jax import lax

D = 2048
HEADS = 16
KVH = 4
HD = 128
HID = 384
TOP = 8
REQ_DEV = 128
CACHE = 64
TOKENS = 4096
SLOTS = 128
EXPERTS = 64
MOST = 24
N_REQ = 32


def key_front(key):
    return jnp.clip(jax.random.normal(jax.random.fold_in(key, 102), (TOKENS, KVH, 1, HD), jnp.float32), -6.0, 6.0)


def draw_keys(key, part):
    first = key_front(key)
    rest = jnp.clip(jax.random.normal(jax.random.fold_in(key, 104), (TOKENS, KVH, CACHE - 1, HD), jnp.float32), -6.0, 6.0)
    return jnp.concatenate([first, rest], axis=2).astype(jnp.bfloat16)


def draw_queries(key, part):
    query = jnp.clip(jax.random.normal(jax.random.fold_in(key, 103), (TOKENS, HEADS, HD), jnp.float32), -6.0, 6.0)
    return query.reshape(TOKENS, HEADS * HD).astype(jnp.bfloat16)


def draw_residual(key, part):
    base = jnp.clip(jax.random.normal(jax.random.fold_in(key, 401), (TOKENS, D), jnp.float32), -6.0, 6.0)
    row_scale = jnp.exp(jax.random.uniform(jax.random.fold_in(key, 402), (TOKENS, 1), jnp.float32, jnp.log(0.3), jnp.log(3.0)))
    col_scale = jnp.exp(jax.random.uniform(jax.random.fold_in(key, 403), (1, D), jnp.float32, jnp.log(0.3), jnp.log(3.0)))
    return (base * row_scale * col_scale).astype(jnp.bfloat16)


def load_order(key):
    return jax.random.permutation(jax.random.fold_in(key, 500), EXPERTS).astype(jnp.int32)


def block_routes(key, block_index, order):
    block_key = jax.random.fold_in(jax.random.fold_in(key, 501), block_index)
    n_entry = EXPERTS * MOST
    entry = jnp.arange(n_entry, dtype=jnp.int32)
    ranked = entry // MOST
    copy_index = entry % MOST
    weight_copy = jnp.where(ranked >= EXPERTS // 2, 3, 1).astype(jnp.int32)
    noise = jax.random.randint(block_key, (n_entry,), 0, 65536, jnp.int32)
    score = noise + copy_index * 16384 * weight_copy
    n_blocks = TOKENS // REQ_DEV
    cold_pick = EXPERTS // 2 + block_index % (EXPERTS - EXPERTS // 2)
    forced = (ranked == 0) | (ranked == cold_pick) | (copy_index == 0) & (ranked % n_blocks == block_index)
    score = jnp.where(forced, -1, score).astype(jnp.int32)
    picked = jnp.argsort(score, stable=True)[:REQ_DEV * TOP].astype(jnp.int32)
    picked = jnp.sort(picked)
    grid = order[picked // MOST].reshape(TOP, REQ_DEV).T
    shuffle = jax.random.permutation(jax.random.fold_in(block_key, 7), REQ_DEV)
    return grid[shuffle].astype(jnp.int32)


def draw_expert_ids(key, part):
    order = load_order(key)
    n_blocks = TOKENS // REQ_DEV
    blocks = jax.vmap(lambda index: block_routes(key, index, order))(jnp.arange(n_blocks, dtype=jnp.int32))
    return blocks.reshape(TOKENS, TOP).astype(jnp.int32)


def replica_table(key):
    order = load_order(key)
    hottest = order[:EXPERTS // 2]
    table = jnp.concatenate([order, hottest, hottest])
    shuffle = jax.random.permutation(jax.random.fold_in(key, 204), SLOTS)
    return table[shuffle].astype(jnp.int32)


def draw_replica_map(key, part):
    return replica_table(key)


def draw_w_gate(key, part):
    base = (jax.random.normal(jax.random.fold_in(key, 301), (EXPERTS, D, HID), jnp.float32) * D ** (-0.5)).astype(jnp.bfloat16)
    return base[replica_table(key)]


def draw_w_up(key, part):
    base = (jax.random.normal(jax.random.fold_in(key, 302), (EXPERTS, D, HID), jnp.float32) * D ** (-0.5)).astype(jnp.bfloat16)
    return base[replica_table(key)]


def draw_w_down(key, part):
    base = (jax.random.normal(jax.random.fold_in(key, 303), (EXPERTS, HID, D), jnp.float32) * HID ** (-0.5)).astype(jnp.bfloat16)
    return base[replica_table(key)]


def with_ends(entries, stream_key, least, largest):
    longest = entries.shape.index(max(entries.shape))
    spots = []
    for shift in (0, 1):
        where = [jax.random.randint(jax.random.fold_in(stream_key, axis), (), 0, length) for axis, length in enumerate(entries.shape)]
        where[longest] = (where[longest] + shift) % entries.shape[longest]
        spots.append(tuple(where))
    return entries.at[spots[0]].set(least).at[spots[1]].set(largest)


def block_levels(key, dims, pieces, least, high):
    def one(axis_at, blocks):
        heights = jax.random.uniform(jax.random.fold_in(jax.random.fold_in(key, 6), axis_at), (blocks,), jnp.float32, least / len(pieces), high / len(pieces))
        return jnp.repeat(jnp.exp(heights), dims[axis_at] // blocks).reshape((-1,) + (1,) * (len(dims) - axis_at - 1))

    loudness = one(*pieces[0])
    for cut in pieces[1:]:
        loudness = loudness * one(*cut)
    return loudness


def bell_draw(rng, dims, width, most, cuts=(), kind=jnp.bfloat16):
    entries = width * jax.random.normal(rng, dims, jnp.float32)
    if cuts:
        entries = entries * block_levels(rng, dims, cuts, -0.22, 0.18)
    return jnp.clip(entries, -most, most).astype(kind)


def setup_inputs(seed: int = 0) -> dict:
    key_of = jax.random.split(jax.random.key(seed), 14)
    queries = draw_queries(jax.random.fold_in(key_of[13], 71), 0)
    keys = draw_keys(jax.random.fold_in(key_of[13], 71), 0)
    values = bell_draw(key_of[2], (TOKENS, KVH, CACHE, HD), 1.0, 6.0, ((0, 64), (1, 4)))
    lengths = with_ends(jax.random.randint(key_of[3], (TOKENS,), 2, CACHE + 1), jax.random.fold_in(key_of[3], 1), 2, CACHE).astype(jnp.int32)
    out_weight = bell_draw(key_of[4], (HEADS * HD, D), (HEADS * HD) ** -0.5, 0.125, ((0, 8),))
    residual = draw_residual(jax.random.fold_in(key_of[13], 71), 0)
    norm_gain = jnp.clip(jnp.exp(jax.random.uniform(key_of[6], (D,), jnp.float32, math.log(0.5), math.log(2.0))), 0.5, 2.0)
    expert_ids = draw_expert_ids(jax.random.fold_in(key_of[13], 71), 0)
    gate_weights = jnp.clip(jnp.exp(math.log(1.0) - 1.609438 * jax.random.uniform(key_of[8], (TOKENS, TOP), jnp.float32) ** block_levels(key_of[8], (TOKENS, TOP), ((0, 32),), -0.2, 0.2)), 0.2, 1.0)
    replica_map = draw_replica_map(jax.random.fold_in(key_of[13], 71), 0)
    w_gate = draw_w_gate(jax.random.fold_in(key_of[13], 71), 0)
    w_up = draw_w_up(jax.random.fold_in(key_of[13], 71), 0)
    w_down = draw_w_down(jax.random.fold_in(key_of[13], 71), 0)
    return dict(queries=queries, keys=keys, values=values, lengths=lengths, out_weight=out_weight, residual=residual, norm_gain=norm_gain, expert_ids=expert_ids, gate_weights=gate_weights, replica_map=replica_map, w_gate=w_gate, w_up=w_up, w_down=w_down)


def reference(queries, keys, values, lengths, out_weight, residual, norm_gain, expert_ids, gate_weights, replica_map, w_gate, w_up, w_down):
    f32 = jnp.float32
    n_tok = queries.shape[0]
    group = HEADS // KVH
    query = queries.astype(f32).reshape(n_tok, KVH, group, HD)
    scores = jnp.einsum('tgqd,tgpd->tgqp', query, keys.astype(f32), precision=lax.Precision.HIGHEST) * HD ** (-0.5)
    position = jnp.arange(CACHE, dtype=jnp.int32)
    valid = (position[None, :] < lengths[:, None])[:, None, None, :]
    scores = jnp.where(valid, scores, -1e+30)
    peak = lax.optimization_barrier(jnp.max(scores, axis=-1, keepdims=True))
    weights = jnp.where(valid, jnp.exp(scores - peak), 0.0)
    probs = weights / lax.optimization_barrier(jnp.sum(weights, axis=-1, keepdims=True))
    attended = jnp.einsum('tgqp,tgpd->tgqd', probs, values.astype(f32), precision=lax.Precision.HIGHEST)
    attended = attended.astype(jnp.bfloat16).reshape(n_tok, HEADS * HD)
    attn_out = jnp.dot(attended, out_weight, preferred_element_type=f32)
    mixed = residual.astype(f32) + attn_out
    scale = lax.rsqrt(lax.optimization_barrier(jnp.mean(mixed * mixed, axis=1)) + 1e-06)
    normed = (mixed * scale[:, None] * norm_gain[None, :]).astype(jnp.bfloat16)
    probs_top = gate_weights / lax.optimization_barrier(jnp.sum(gate_weights, axis=1, keepdims=True))
    flat_ids = expert_ids.reshape(-1)
    n_pairs = flat_ids.shape[0]
    flat_probs = jnp.concatenate([probs_top.reshape(-1), jnp.zeros((1,), f32)])
    flat_rows = jnp.concatenate([jnp.arange(n_pairs, dtype=jnp.int32) // TOP, jnp.full((1,), n_tok, jnp.int32)])
    padded = jnp.concatenate([normed, jnp.zeros((1, D), jnp.bfloat16)], axis=0)
    bound = MOST * N_REQ
    half = HID // 2

    def one_expert(moe, expert):
        chosen = jnp.nonzero(flat_ids == expert, size=bound, fill_value=n_pairs)[0].astype(jnp.int32)
        rows_idx = flat_rows[chosen]
        weight = flat_probs[chosen]
        slot = jnp.argmax(replica_map == expert).astype(jnp.int32)
        rows = padded[rows_idx]
        gate = jnp.dot(rows, w_gate[slot], preferred_element_type=f32)
        up = jnp.dot(rows, w_up[slot], preferred_element_type=f32)
        act = (jax.nn.silu(gate) * up).astype(jnp.bfloat16)
        down = w_down[slot]
        low = jnp.dot(act[:, :half], down[:half], preferred_element_type=f32).astype(jnp.bfloat16)
        high = jnp.dot(act[:, half:], down[half:], preferred_element_type=f32).astype(jnp.bfloat16)
        low = lax.optimization_barrier(low)
        high = lax.optimization_barrier(high)
        out = (low.astype(f32) + high.astype(f32)).astype(jnp.bfloat16)
        out = lax.optimization_barrier(out)
        moe = moe.at[rows_idx].add(out.astype(f32) * weight[:, None], mode='drop')
        return (moe, None)
    moe, _ = lax.scan(one_expert, jnp.zeros((n_tok, D), f32), jnp.arange(EXPERTS, dtype=jnp.int32))
    return (mixed + moe).astype(jnp.bfloat16)
```

```python
import jax
import jax.numpy as jnp
from jax import lax
from jax.experimental import pallas as pl
from jax.experimental.pallas import tpu as pltpu
from jax.sharding import PartitionSpec as P

MESH = pl.DeviceIdType.MESH
F32 = jnp.float32
BF16 = jnp.bfloat16

NZ = 8
CAP = 24
ORDER = (0, 1, 4, 5, 3, 6, 2, 7)
PAIRS = NZ // 2


def layer_kernel(
    q_ref,
    len_ref,
    gain_ref,
    route_ref,
    map_ref,
    k_hbm,
    v_hbm,
    ow_hbm,
    res_hbm,
    wg_hbm,
    wu_hbm,
    wd_hbm,
    out_ref,
    kbuf,
    vbuf,
    owb,
    resb,
    lens_t,
    eprim,
    att,
    oh,
    rs_send,
    rs_recv,
    mixed,
    sq_send,
    sq_recv,
    sc,
    rt,
    xg,
    dmat,
    wmat,
    send1,
    recv1,
    send2,
    recv2,
    own_sum,
    zs_send,
    zs_recv,
    wg,
    wu,
    wd,
    load_sem,
    w_send,
    w_in,
    fwd_send,
    w_other,
    att_sems,
    rs_sems,
    sq_sems,
    sc_send,
    sc_recv,
    rt_send,
    rt_recv,
    xg_send,
    xg_recv,
    a2a_send,
    a2a_recv,
    back_send,
    back_recv,
    zs_sems,
):
    req = lax.axis_index("req")
    y = lax.axis_index("kvh")
    xl = lax.axis_index("exp")
    z = lax.div(req, 4)
    xh = lax.rem(lax.div(req, 2), 2)
    c = lax.rem(req, 2)
    blk = y * 2 + xl
    slot = xh * 8 + xl * 4 + y
    swap = lax.rem(c + xl, 2)

    def plane_peer(d):
        xh_to = lax.rem(xh + lax.div(d, 8), 2)
        xl_to = lax.rem(xl + lax.rem(lax.div(d, 4), 2), 2)
        y_to = lax.rem(y + lax.rem(d, 4), 4)
        return xh_to, xl_to, y_to, (z * 4 + xh_to * 2 + c, y_to, xl_to)

    def z_peer(d):
        return (lax.rem(z + d, NZ) * 4 + xh * 2 + c, y, xl)

    other_core = (z * 4 + xh * 2 + (1 - c), y, xl)
    swap_peer = (z * 4 + xh * 2 + (1 - c), y, 1 - xl)

    barrier = pltpu.get_barrier_semaphore()

    def greet_plane(d, carry):
        pl.semaphore_signal(barrier, inc=1, device_id=plane_peer(d)[3], device_id_type=MESH)
        return carry

    lax.fori_loop(1, 16, greet_plane, 0)

    def greet_z(d, carry):
        pl.semaphore_signal(barrier, inc=1, device_id=z_peer(d), device_id_type=MESH)
        return carry

    lax.fori_loop(1, NZ, greet_z, 0)
    pl.semaphore_signal(barrier, inc=1, device_id=other_core, device_id_type=MESH)

    @pl.when(swap == 1)
    def _():
        pl.semaphore_signal(barrier, inc=1, device_id=swap_peer, device_id_type=MESH)

    def load(src, dst, i):
        return pltpu.make_async_copy(src, dst, load_sem.at[i])

    loads = [load(k_hbm, kbuf, 0), load(v_hbm, vbuf, 1)]
    loads.append(
        load(res_hbm.at[:, pl.ds(pl.multiple_of(blk * 256, 256), 256)], resb, 2)
    )
    for b in range(8):
        loads.append(load(ow_hbm.at[:, pl.ds(b * 256, 256)], owb.at[b], 3 + b))
    for one in loads:
        one.start()
    pl.semaphore_wait(barrier, 23 + swap)

    weights = ((wg_hbm, wg), (wu_hbm, wu), (wd_hbm, wd))

    def remote(src, dst, send_sem, recv_sem, device):
        return pltpu.make_async_remote_copy(
            src_ref=src,
            dst_ref=dst,
            send_sem=send_sem,
            recv_sem=recv_sem,
            device_id=device,
            device_id_type=MESH,
        )

    rt[0] = route_ref[...]
    for pos in range(1, NZ):
        remote(
            rt.at[0], rt.at[pos], rt_send.at[pos], rt_recv.at[pos], z_peer(NZ - ORDER[pos])
        ).start()

    @pl.when(swap == 0)
    def _():
        for i, (src, dst) in enumerate(weights):
            pltpu.make_async_copy(src, dst.at[c], w_in.at[i]).start()
            remote(src, dst.at[c], w_send.at[i], w_other.at[i], other_core).start()

    @pl.when(swap == 1)
    def _():
        for i, (src, dst) in enumerate(weights):
            remote(src, dst.at[1 - c], w_send.at[i], w_in.at[i], swap_peer).start()

    lens_t[...] = jnp.broadcast_to(len_ref[...].astype(F32), (128, 128)).T
    loads[0].wait()
    loads[1].wait()
    scale = 128 ** (-0.5)
    rows_at = lax.broadcasted_iota(jnp.int32, (64, 1024), 0)
    cols_at = lax.broadcasted_iota(jnp.int32, (64, 1024), 1)
    same = (rows_at & 15) == (cols_at >> 6)
    at = (cols_at & 63).astype(F32)
    for g in range(4):
        lo = g * 16
        heads = [q_ref[lo : lo + 16, h * 128 : (h + 1) * 128] for h in range(4)]
        q16 = jnp.concatenate(heads, axis=0)
        k16 = kbuf[g * 1024 : (g + 1) * 1024, :]
        s = lax.dot_general(q16, k16, (((1,), (1,)), ((), ())), preferred_element_type=F32)
        own_len = lens_t[pl.ds(pl.multiple_of(xl * 64 + lo, 16), 16), :][:, 0:1]
        live = same & (at < jnp.concatenate([own_len] * 4, axis=0))
        s = jnp.where(live, s * scale, -1e30)
        peak = jnp.max(s, axis=1, keepdims=True)
        w = jnp.where(live, jnp.exp(s - peak), 0.0)
        total = jnp.sum(w, axis=1, keepdims=True)
        v16 = vbuf[g * 1024 : (g + 1) * 1024, :]
        a = jnp.dot(w.astype(BF16), v16, preferred_element_type=F32) / total
        a = a.astype(BF16)
        for h in range(4):
            att[h // 2, lo : lo + 16, (h % 2) * 128 : (h % 2 + 1) * 128] = a[
                h * 16 : (h + 1) * 16, :
            ]
    att_copy = remote(
        att.at[1 - xl], oh.at[xl], att_sems.at[0], att_sems.at[1], (req, y, 1 - xl)
    )
    att_copy.start()
    oh[xl] = att[xl]

    row = jnp.broadcast_to(map_ref[...].astype(F32), (128, 128))
    col = row.T
    sub = lax.broadcasted_iota(jnp.int32, (128, 128), 0)
    lane = lax.broadcasted_iota(jnp.int32, (128, 128), 1)
    again = jnp.where((row == col) & (lane < sub), 1.0, 0.0)
    eprim[...] = jnp.where(jnp.max(again, axis=1, keepdims=True) > 0.0, -1.0, col)

    for i in range(2, 11):
        loads[i].wait()
    att_copy.wait()
    heads_all = oh[...].reshape(128, 256)

    def scatter(d, carry):
        to = lax.rem(blk + d, 8)
        part = jnp.dot(heads_all, owb[to], preferred_element_type=F32)
        rs_send[d - 1] = part.astype(BF16)
        remote(
            rs_send.at[d - 1],
            rs_recv.at[d - 1],
            rs_sems.at[0],
            rs_sems.at[1],
            (req, lax.div(to, 2), lax.rem(to, 2)),
        ).start()
        return carry

    lax.fori_loop(1, 8, scatter, 0)
    own_part = jnp.dot(heads_all, owb[blk], preferred_element_type=F32)

    for pos in range(1, NZ):
        remote(rt.at[0], rt.at[pos], rt_send.at[pos], rt_recv.at[pos], z_peer(NZ - ORDER[pos])).wait()
    expert = eprim[pl.ds(pl.multiple_of(z * 16, 16), 16), :]
    upper = jnp.where(sub < lane, 1.0, 0.0).astype(BF16)
    kk = lax.broadcasted_iota(jnp.int32, (2 * CAP, 256), 0).astype(F32)

    def routing(p, carry):
        places, probs = [], []
        for r in range(2):
            info = rt[2 * p + r]
            ids = info[0:8, :]
            gates = info[8:16, :]
            top = gates / jnp.sum(gates, axis=0, keepdims=True)
            named = jnp.zeros((16, 128), F32)
            prob = jnp.zeros((16, 128), F32)
            for j in range(8):
                hit = ids[j : j + 1, :] == expert
                named = jnp.where(hit, 1.0, named)
                prob = jnp.where(hit, top[j : j + 1, :], prob)
            before = jnp.dot(named.astype(BF16), upper, preferred_element_type=F32)
            places.append(jnp.where(named > 0.0, before + r * CAP, -100.0))
            probs.append(prob)
        place = jnp.concatenate(places, axis=1)
        prob = jnp.concatenate(probs, axis=1)
        for s in range(16):
            chosen = place[s : s + 1, :] == kk
            dmat[p, s] = jnp.where(chosen, 1.0, 0.0).astype(BF16)
            wmat[p, s] = jnp.where(chosen, prob[s : s + 1, :], 0.0).astype(BF16)
        return carry

    lax.fori_loop(0, PAIRS, routing, 0)

    pltpu.make_async_copy(rs_recv, rs_recv, rs_sems.at[1]).wait()
    total = resb[...].astype(F32) + own_part
    for d in range(7):
        total = total + rs_recv[d].astype(F32)
    mixed[...] = total
    gain = gain_ref[:, pl.ds(pl.multiple_of(blk * 256, 256), 256)]
    xg[0] = (total * gain).astype(BF16)
    sq_send[...] = lax.dot_general(
        jnp.ones((8, 256), F32),
        total * total,
        (((1,), (1,)), ((), ())),
        preferred_element_type=F32,
        precision=lax.Precision.HIGHEST,
    )

    def share_squares(d, carry):
        to = lax.rem(blk + d, 8)
        remote(
            sq_send,
            sq_recv.at[d - 1],
            sq_sems.at[0],
            sq_sems.at[1],
            (req, lax.div(to, 2), lax.rem(to, 2)),
        ).start()
        return carry

    lax.fori_loop(1, 8, share_squares, 0)
    for pos in range(1, NZ):
        remote(
            xg.at[0], xg.at[pos], xg_send.at[pos], xg_recv.at[pos], z_peer(NZ - ORDER[pos])
        ).start()
    pltpu.make_async_copy(sq_recv, sq_recv, sq_sems.at[1]).wait()
    squares = sq_send[...]
    for d in range(7):
        squares = squares + sq_recv[d]
    sc[0] = lax.rsqrt(squares * (1.0 / 2048.0) + 1e-6)
    for pos in range(1, NZ):
        remote(
            sc.at[0], sc.at[pos], sc_send.at[pos], sc_recv.at[pos], z_peer(NZ - ORDER[pos])
        ).start()

    for p in range(PAIRS):
        scaled = []
        for pos in (2 * p, 2 * p + 1):
            if pos:
                device = z_peer(NZ - ORDER[pos])
                remote(xg.at[0], xg.at[pos], xg_send.at[pos], xg_recv.at[pos], device).wait()
                remote(sc.at[0], sc.at[pos], sc_send.at[pos], sc_recv.at[pos], device).wait()
            factor = jnp.broadcast_to(sc[pos, 0:1, :], (128, 128)).T
            both = jnp.concatenate([factor, factor], axis=1)
            scaled.append((xg[pos].astype(F32) * both).astype(BF16))
        rows = jnp.concatenate(scaled, axis=0)
        picked = jnp.dot(dmat[p].reshape(768, 256), rows, preferred_element_type=F32)
        send1[p] = picked.astype(BF16).reshape(16, 2 * CAP, 256)

        def dispatch(d, carry, p=p):
            xh_to, xl_to, y_to, device = plane_peer(d)
            remote(
                send1.at[p, xh_to * 8 + xl_to * 4 + y_to],
                recv1.at[p, blk, xh],
                a2a_send.at[p],
                a2a_recv.at[p],
                device,
            ).start()
            return carry

        lax.fori_loop(1, 16, dispatch, 0)
        pltpu.make_async_copy(send1.at[p, slot], recv1.at[p, blk, xh], a2a_recv.at[p]).start()

    for i, (_, dst) in enumerate(weights):
        pltpu.make_async_copy(dst.at[c], dst.at[c], w_in.at[i]).wait()

    @pl.when(swap == 1)
    def _():
        for i, (_, dst) in enumerate(weights):
            remote(dst.at[c], dst.at[c], fwd_send.at[i], w_other.at[i], other_core).start()

    for i, (_, dst) in enumerate(weights):
        pltpu.make_async_copy(dst.at[1 - c], dst.at[1 - c], w_other.at[i]).wait()

    for p in range(PAIRS):
        pltpu.make_async_copy(recv1.at[p], recv1.at[p], a2a_recv.at[p]).wait()
        rows = jnp.concatenate(
            [recv1[p, b].reshape(4 * CAP, 256) for b in range(8)], axis=1
        )
        out = None
        for half in range(2):
            gate = jnp.dot(rows, wg[half], preferred_element_type=F32)
            up = jnp.dot(rows, wu[half], preferred_element_type=F32)
            act = (gate / (1.0 + jnp.exp(-gate)) * up).astype(BF16)
            down = jnp.dot(act, wd[half], preferred_element_type=F32)
            out = down if out is None else out + down
        for b in range(8):
            piece = out[:, b * 256 : (b + 1) * 256].astype(BF16)
            send2[p, b] = piece.reshape(2, 2 * CAP, 256)

        def give_back(d, carry, p=p):
            xh_to, xl_to, y_to, device = plane_peer(d)
            remote(
                send2.at[p, y_to * 2 + xl_to, xh_to],
                recv2.at[p, slot],
                back_send.at[p],
                back_recv.at[p],
                device,
            ).start()
            return carry

        lax.fori_loop(1, 16, give_back, 0)
        pltpu.make_async_copy(send2.at[p, blk, xh], recv2.at[p, slot], back_recv.at[p]).start()

    for p in range(PAIRS):
        pltpu.make_async_copy(recv2.at[p], recv2.at[p], back_recv.at[p]).wait()
        part = lax.dot_general(
            wmat[p].reshape(768, 256),
            recv2[p].reshape(768, 256),
            (((0,), (0,)), ((), ())),
            preferred_element_type=F32,
        )
        for r in range(2):
            pos = 2 * p + r
            piece = part[r * 128 : (r + 1) * 128, :]
            if pos == 0:
                own_sum[...] = piece
            else:
                zs_send[pos - 1] = piece.astype(BF16)
                remote(
                    zs_send.at[pos - 1],
                    zs_recv.at[pos - 1],
                    zs_sems.at[0],
                    zs_sems.at[1],
                    z_peer(ORDER[pos]),
                ).start()
    pltpu.make_async_copy(zs_recv, zs_recv, zs_sems.at[1]).wait()
    total = mixed[...] + own_sum[...]
    for d in range(7):
        total = total + zs_recv[d].astype(F32)
    out_ref[...] = total.astype(BF16)

    pltpu.make_async_copy(rs_send, rs_send, rs_sems.at[0]).wait()
    pltpu.make_async_copy(sq_recv, sq_recv, sq_sems.at[0]).wait()
    pltpu.make_async_copy(zs_send, zs_send, zs_sems.at[0]).wait()
    for p in range(PAIRS):
        sent = send1.at[p, pl.ds(0, 15)]
        pltpu.make_async_copy(sent, sent, a2a_send.at[p]).wait()
        sent = recv2.at[p, pl.ds(0, 15)]
        pltpu.make_async_copy(sent, sent, back_send.at[p]).wait()
    for i, (src, dst) in enumerate(weights):
        pltpu.make_async_copy(dst.at[c], dst.at[c], w_send.at[i]).wait()

    @pl.when(swap == 1)
    def _():
        for i, (_, dst) in enumerate(weights):
            pltpu.make_async_copy(dst.at[c], dst.at[c], fwd_send.at[i]).wait()


def shards(
    queries,
    keys,
    values,
    lengths,
    out_weight,
    residual,
    norm_gain,
    expert_ids,
    gate_weights,
    replica_map,
    w_gate,
    w_up,
    w_down,
):
    route = jnp.concatenate([expert_ids.T.astype(F32), gate_weights.T], axis=0)
    vmem = pl.BlockSpec(memory_space=pltpu.VMEM)
    hbm = pl.BlockSpec(memory_space=pl.ANY)
    dma = pltpu.SemaphoreType.DMA
    return pl.pallas_call(
        layer_kernel,
        out_shape=jax.ShapeDtypeStruct((128, 256), BF16),
        in_specs=[vmem] * 5 + [hbm] * 7,
        out_specs=vmem,
        scratch_shapes=[
            pltpu.VMEM((4096, 128), BF16),
            pltpu.VMEM((4096, 128), BF16),
            pltpu.VMEM((8, 256, 256), BF16),
            pltpu.VMEM((128, 256), BF16),
            pltpu.VMEM((128, 128), F32),
            pltpu.VMEM((128, 128), F32),
            pltpu.VMEM((2, 64, 256), BF16),
            pltpu.VMEM((2, 64, 256), BF16),
            pltpu.VMEM((7, 128, 256), BF16),
            pltpu.VMEM((7, 128, 256), BF16),
            pltpu.VMEM((128, 256), F32),
            pltpu.VMEM((8, 128), F32),
            pltpu.VMEM((7, 8, 128), F32),
            pltpu.VMEM((8, 8, 128), F32),
            pltpu.VMEM((8, 16, 128), F32),
            pltpu.VMEM((8, 128, 256), BF16),
            pltpu.VMEM((PAIRS, 16, 2 * CAP, 256), BF16),
            pltpu.VMEM((PAIRS, 16, 2 * CAP, 256), BF16),
            pltpu.VMEM((PAIRS, 16, 2 * CAP, 256), BF16),
            pltpu.VMEM((PAIRS, 8, 2, 2 * CAP, 256), BF16),
            pltpu.VMEM((PAIRS, 8, 2, 2 * CAP, 256), BF16),
            pltpu.VMEM((PAIRS, 16, 2 * CAP, 256), BF16),
            pltpu.VMEM((128, 256), F32),
            pltpu.VMEM((7, 128, 256), BF16),
            pltpu.VMEM((7, 128, 256), BF16),
            pltpu.VMEM((2, 2048, 192), BF16),
            pltpu.VMEM((2, 2048, 192), BF16),
            pltpu.VMEM((2, 192, 2048), BF16),
            dma((11,)),
            dma((3,)),
            dma((3,)),
            dma((3,)),
            dma((3,)),
            dma((2,)),
            dma((2,)),
            dma((2,)),
            dma((8,)),
            dma((8,)),
            dma((8,)),
            dma((8,)),
            dma((8,)),
            dma((8,)),
            dma((PAIRS,)),
            dma((PAIRS,)),
            dma((PAIRS,)),
            dma((PAIRS,)),
            dma((2,)),
        ],
        compiler_params=pltpu.CompilerParams(
            collective_id=0, has_side_effects=True, vmem_limit_bytes=56 * 2**20
        ),
        name="layer",
    )(
        queries,
        lengths.reshape(1, 128),
        norm_gain.reshape(1, 2048),
        route,
        replica_map.reshape(1, 128),
        keys.reshape(4096, 128),
        values.reshape(4096, 128),
        out_weight,
        residual,
        w_gate.reshape(2048, 192),
        w_up.reshape(2048, 192),
        w_down.reshape(192, 2048),
    )


def solution(mesh):
    in_specs = (
        P(("req", "exp"), "kvh"),
        P(("req", "exp"), "kvh", None, None),
        P(("req", "exp"), "kvh", None, None),
        P("req"),
        P(("kvh", "exp"), None),
        P("req", None),
        P(),
        P("req", None),
        P("req", None),
        P(),
        P(("req", "kvh"), None, "exp"),
        P(("req", "kvh"), None, "exp"),
        P(("req", "kvh"), "exp", None),
    )
    out_specs = P("req", ("kvh", "exp"))
    return jax.shard_map(shards, mesh=mesh, in_specs=in_specs, out_specs=out_specs, check_vma=False)
```

```python
import jax
import jax.numpy as jnp
from jax import lax
from jax.experimental import pallas as pl
from jax.experimental.pallas import tpu as pltpu
from jax.sharding import PartitionSpec as P

MESH = pl.DeviceIdType.MESH
F32 = jnp.float32
BF16 = jnp.bfloat16

NZ = 8
CAP = 24
ORDER = (0, 1, 7, 2, 6, 3, 5, 4)
PAIRS = NZ // 2


def layer_kernel(
    q_ref,
    len_ref,
    gain_ref,
    ids_ref,
    gates_ref,
    map_ref,
    k_hbm,
    v_hbm,
    ow_hbm,
    res_hbm,
    wg_hbm,
    wu_hbm,
    wd_hbm,
    out_ref,
    kbuf,
    vbuf,
    owb,
    resb,
    lens_t,
    eprim,
    att,
    oh,
    rs_send,
    rs_recv,
    mixed,
    sq_send,
    sq_recv,
    xraw,
    rt,
    xg,
    dmat,
    wmat,
    send1,
    recv1,
    send2,
    recv2,
    own_part,
    own_sum,
    xs_send,
    xs_recv,
    zs_send,
    zs_recv,
    wg,
    wu,
    wd,
    load_sem,
    w_send,
    w_in,
    fwd_send,
    w_other,
    att_sems,
    rs_sems,
    sq_sems,
    xraw_sems,
    rt_send,
    rt_recv,
    xg_send,
    xg_recv,
    a2a_send,
    a2a_recv,
    back_send,
    back_recv,
    xs_send_sem,
    xs_recv_sem,
    zs_sems,
):
    req = lax.axis_index("req")
    y = lax.axis_index("kvh")
    xl = lax.axis_index("exp")
    z = lax.div(req, 4)
    xh = lax.rem(lax.div(req, 2), 2)
    c = lax.rem(req, 2)
    blk = y * 2 + xl
    swap = lax.rem(c + xl, 2)

    def serve_peer(d):
        side = lax.div(d, 4)
        xh_to = lax.rem(xh + side, 2)
        xl_to = lax.rem(xl + side, 2)
        y_to = lax.rem(y + d, 4)
        return side, xh_to, y_to, (z * 4 + xh_to * 2 + c, y_to, xl_to)

    def group_peer(d):
        to = lax.rem(blk + d, 8)
        return to, (req, lax.div(to, 2), lax.rem(to, 2))

    def z_peer(d):
        return (lax.rem(z + d, NZ) * 4 + xh * 2 + c, y, xl)

    exp_peer = (req, y, 1 - xl)
    other_core = (z * 4 + xh * 2 + (1 - c), y, xl)
    swap_peer = (z * 4 + xh * 2 + (1 - c), y, 1 - xl)

    def remote(src, dst, send_sem, recv_sem, device):
        return pltpu.make_async_remote_copy(
            src_ref=src,
            dst_ref=dst,
            send_sem=send_sem,
            recv_sem=recv_sem,
            device_id=device,
            device_id_type=MESH,
        )

    barrier = pltpu.get_barrier_semaphore()

    def greet_group(d, carry):
        pl.semaphore_signal(barrier, inc=1, device_id=group_peer(d)[1], device_id_type=MESH)
        pl.semaphore_signal(barrier, inc=1, device_id=z_peer(d), device_id_type=MESH)
        return carry

    lax.fori_loop(1, 8, greet_group, 0)

    def greet_side(d, carry):
        pl.semaphore_signal(barrier, inc=1, device_id=serve_peer(d)[3], device_id_type=MESH)
        return carry

    lax.fori_loop(4, 8, greet_side, 0)
    pl.semaphore_signal(barrier, inc=1, device_id=other_core, device_id_type=MESH)

    @pl.when(swap == 1)
    def _():
        pl.semaphore_signal(barrier, inc=1, device_id=swap_peer, device_id_type=MESH)

    def load(src, dst, i):
        return pltpu.make_async_copy(src, dst, load_sem.at[i])

    loads = [load(k_hbm, kbuf, 0), load(v_hbm, vbuf, 1)]
    loads.append(
        load(res_hbm.at[:, pl.ds(pl.multiple_of(blk * 256, 256), 256)], resb, 2)
    )
    for b in range(8):
        loads.append(load(ow_hbm.at[:, pl.ds(b * 256, 256)], owb.at[b], 3 + b))
    for one in loads:
        one.start()
    rt[0, 0:8, :] = ids_ref[...].astype(F32)
    rt[0, 8:16, :] = gates_ref[...]
    lens_t[...] = jnp.broadcast_to(len_ref[...].astype(F32), (128, 128)).T

    row = jnp.broadcast_to(map_ref[...].astype(F32), (128, 128))
    col = row.T
    sub = lax.broadcasted_iota(jnp.int32, (128, 128), 0)
    lane = lax.broadcasted_iota(jnp.int32, (128, 128), 1)
    again = jnp.where((row == col) & (lane < sub), 1.0, 0.0)
    eprim[...] = jnp.where(jnp.max(again, axis=1, keepdims=True) > 0.0, -1.0, col)

    loads[0].wait()
    loads[1].wait()
    scale = 128 ** (-0.5)
    rows_at = lax.broadcasted_iota(jnp.int32, (64, 1024), 0)
    cols_at = lax.broadcasted_iota(jnp.int32, (64, 1024), 1)
    same = (rows_at & 15) == (cols_at >> 6)
    at = (cols_at & 63).astype(F32)
    for g in range(4):
        lo = g * 16
        heads = [q_ref[lo : lo + 16, h * 128 : (h + 1) * 128] for h in range(4)]
        q16 = jnp.concatenate(heads, axis=0)
        k16 = kbuf[g * 1024 : (g + 1) * 1024, :]
        s = lax.dot_general(q16, k16, (((1,), (1,)), ((), ())), preferred_element_type=F32)
        own_len = lens_t[pl.ds(pl.multiple_of(xl * 64 + lo, 16), 16), :][:, 0:1]
        live = same & (at < jnp.concatenate([own_len] * 4, axis=0))
        s = jnp.where(live, s * scale, -1e30)
        peak = jnp.max(s, axis=1, keepdims=True)
        w = jnp.where(live, jnp.exp(s - peak), 0.0)
        total = jnp.sum(w, axis=1, keepdims=True)
        v16 = vbuf[g * 1024 : (g + 1) * 1024, :]
        a = jnp.dot(w.astype(BF16), v16, preferred_element_type=F32) / total
        a = a.astype(BF16)
        for h in range(4):
            att[h // 2, lo : lo + 16, (h % 2) * 128 : (h % 2 + 1) * 128] = a[
                h * 16 : (h + 1) * 16, :
            ]
    oh[xl] = att[xl]

    pl.semaphore_wait(barrier, 19 + swap)
    att_copy = remote(att.at[1 - xl], oh.at[xl], att_sems.at[0], att_sems.at[1], exp_peer)
    att_copy.start()

    weights = ((wg_hbm, wg), (wu_hbm, wu), (wd_hbm, wd))

    def swap_pieces(first, last):
        @pl.when(swap == 1)
        def _():
            for piece in range(first, last):
                i, part = piece // 4, pl.ds(piece % 4 * 48, 48)
                src, dst = weights[i]
                remote(
                    src.at[part], dst.at[1 - c, part], w_send.at[i], w_in.at[i], swap_peer
                ).start()

    swap_pieces(0, 1)

    @pl.when(swap == 0)
    def _():
        for i, (src, dst) in enumerate(weights):
            pltpu.make_async_copy(src, dst.at[c], w_in.at[i]).start()
            remote(src, dst.at[c], w_send.at[i], w_other.at[i], other_core).start()

    for pos in range(1, NZ):
        remote(
            rt.at[0], rt.at[pos], rt_send.at[pos], rt_recv.at[pos], z_peer(NZ - ORDER[pos])
        ).start()

    for i in range(2, 11):
        loads[i].wait()
    att_copy.wait()
    heads_all = oh[...].reshape(128, 256)

    def scatter(d, carry):
        to, device = group_peer(d)
        part = jnp.dot(heads_all, owb[to], preferred_element_type=F32)
        rs_send[d - 1] = part.astype(BF16)
        remote(
            rs_send.at[d - 1], rs_recv.at[d - 1], rs_sems.at[0], rs_sems.at[1], device
        ).start()
        return carry

    lax.fori_loop(1, 8, scatter, 0)
    swap_pieces(1, 3)
    own_out = jnp.dot(heads_all, owb[blk], preferred_element_type=F32)

    for pos in range(1, NZ):
        remote(
            rt.at[0], rt.at[pos], rt_send.at[pos], rt_recv.at[pos], z_peer(NZ - ORDER[pos])
        ).wait()
    first_slot = z * 16 + xh * 8 + xl * 4
    side_slot = z * 16 + (1 - xh) * 8 + (1 - xl) * 4
    expert = jnp.concatenate(
        [eprim[pl.ds(first_slot + i, 1), :] for i in range(4)]
        + [eprim[pl.ds(side_slot + i, 1), :] for i in range(4)],
        axis=0,
    )
    upper = jnp.where(sub < lane, 1.0, 0.0).astype(BF16)
    kk = lax.broadcasted_iota(jnp.int32, (2 * CAP, 256), 0).astype(F32)

    def routing(p, carry):
        places, probs = [], []
        for r in range(2):
            info = rt[2 * p + r]
            ids = info[0:8, :]
            gates = info[8:16, :]
            top = gates / jnp.sum(gates, axis=0, keepdims=True)
            named = jnp.zeros((8, 128), F32)
            prob = jnp.zeros((8, 128), F32)
            for j in range(8):
                hit = ids[j : j + 1, :] == expert
                named = jnp.where(hit, 1.0, named)
                prob = jnp.where(hit, top[j : j + 1, :], prob)
            before = jnp.dot(named.astype(BF16), upper, preferred_element_type=F32)
            places.append(jnp.where(named > 0.0, before + r * CAP, -100.0))
            probs.append(prob)
        place = jnp.concatenate(places, axis=1)
        prob = jnp.concatenate(probs, axis=1)
        for s in range(8):
            chosen = place[s : s + 1, :] == kk
            dmat[p, s] = jnp.where(chosen, 1.0, 0.0).astype(BF16)
            wmat[p, s] = jnp.where(chosen, prob[s : s + 1, :], 0.0).astype(BF16)
        return carry

    lax.fori_loop(0, PAIRS, routing, 0)

    pltpu.make_async_copy(rs_recv, rs_recv, rs_sems.at[1]).wait()
    total = resb[...].astype(F32) + own_out
    for d in range(7):
        total = total + rs_recv[d].astype(F32)
    mixed[...] = total
    sq_send[...] = lax.dot_general(
        jnp.ones((8, 256), F32),
        total * total,
        (((1,), (1,)), ((), ())),
        preferred_element_type=F32,
        precision=lax.Precision.HIGHEST,
    )

    def share_squares(d, carry):
        remote(
            sq_send, sq_recv.at[d - 1], sq_sems.at[0], sq_sems.at[1], group_peer(d)[1]
        ).start()
        return carry

    lax.fori_loop(1, 8, share_squares, 0)
    gain = gain_ref[:, pl.ds(pl.multiple_of(blk * 256, 256), 256)]
    xraw[xl] = (total * gain).astype(BF16)
    xraw_copy = remote(xraw.at[xl], xraw.at[xl], xraw_sems.at[0], xraw_sems.at[1], exp_peer)
    xraw_copy.start()
    swap_pieces(3, 12)
    pltpu.make_async_copy(sq_recv, sq_recv, sq_sems.at[1]).wait()
    squares = sq_send[...]
    for d in range(7):
        squares = squares + sq_recv[d]
    factor = lax.rsqrt(squares * (1.0 / 2048.0) + 1e-6)
    factor = jnp.broadcast_to(factor[0:1, :], (128, 128)).T
    factor = jnp.concatenate([factor, factor], axis=1)
    xraw_copy.wait()
    for half in range(2):
        xg[0, half] = (xraw[half].astype(F32) * factor).astype(BF16)

    def onward(pos_from, pos_to, step):
        return remote(
            xg.at[pos_from], xg.at[pos_to], xg_send.at[pos_to], xg_recv.at[pos_to], z_peer(step)
        )

    place_of = {offset: pos for pos, offset in enumerate(ORDER)}
    hops = {}
    for k in range(4):
        hops[place_of[k + 1]] = onward(place_of[k], place_of[k + 1], NZ - 1)
    for k in range(3):
        hops[place_of[NZ - 1 - k]] = onward(
            place_of[(NZ - k) % NZ], place_of[NZ - 1 - k], 1
        )
    hops[1].start()
    hops[2].start()

    for p in range(PAIRS):
        for pos in (2 * p + 1, 2 * p + 2):
            if pos < NZ:
                hops[pos].wait_recv()
                if pos + 2 < NZ:
                    hops[pos + 2].start()
        for half in range(2):
            rows = xg[2 * p : 2 * p + 2, half].reshape(256, 256)
            picked = jnp.dot(dmat[p].reshape(384, 256), rows, preferred_element_type=F32)
            send1[p, :, :, half * 256 : (half + 1) * 256] = picked.astype(BF16).reshape(
                8, 2 * CAP, 256
            )

        def dispatch(d, carry, p=p):
            side, _, y_to, device = serve_peer(d)
            remote(
                send1.at[p, side * 4 + y_to],
                recv1.at[p, y, xh],
                a2a_send.at[p],
                a2a_recv.at[p],
                device,
            ).start()
            return carry

        lax.fori_loop(1, 8, dispatch, 0)
        pltpu.make_async_copy(send1.at[p, y], recv1.at[p, y, xh], a2a_recv.at[p]).start()

    for i, (_, dst) in enumerate(weights):
        pltpu.make_async_copy(dst.at[c], dst.at[c], w_in.at[i]).wait()

        @pl.when(swap == 1)
        def _(i=i, dst=dst):
            remote(dst.at[c], dst.at[c], fwd_send.at[i], w_other.at[i], other_core).start()

    for i, (_, dst) in enumerate(weights):
        pltpu.make_async_copy(dst.at[1 - c], dst.at[1 - c], w_other.at[i]).wait()

    contract = (((1,), (1,)), ((), ()))
    for p in reversed(range(PAIRS)):
        pltpu.make_async_copy(recv1.at[p], recv1.at[p], a2a_recv.at[p]).wait()
        rows = jnp.concatenate(
            [recv1[p, b].reshape(4 * CAP, 512) for b in range(4)], axis=1
        )
        out = None
        for half in range(2):
            gate = lax.dot_general(rows, wg[half], contract, preferred_element_type=F32)
            up = lax.dot_general(rows, wu[half], contract, preferred_element_type=F32)
            act = (gate / (1.0 + jnp.exp(-gate)) * up).astype(BF16)
            down = jnp.dot(act, wd[half], preferred_element_type=F32)
            out = down if out is None else out + down
        for b in range(4):
            piece = out[:, b * 512 : (b + 1) * 512].astype(BF16)
            send2[p, b] = piece.reshape(2, 2 * CAP, 512)

        def give_back(d, carry, p=p):
            side, xh_to, y_to, device = serve_peer(d)
            remote(
                send2.at[p, y_to, xh_to],
                recv2.at[p, side * 4 + y],
                back_send.at[p],
                back_recv.at[p],
                device,
            ).start()
            return carry

        lax.fori_loop(1, 8, give_back, 0)
        pltpu.make_async_copy(send2.at[p, y, xh], recv2.at[p, y], back_recv.at[p]).start()

    def xs_copy(p):
        return remote(
            xs_send.at[p], xs_recv.at[p], xs_send_sem.at[p], xs_recv_sem.at[p], exp_peer
        )

    def to_owner(p):
        xs_copy(p).wait_recv()
        for r in range(2):
            pos = 2 * p + r
            piece = own_part[p, r] + xs_recv[p, r].astype(F32)
            if pos == 0:
                own_sum[...] = piece
            else:
                zs_send[pos - 1] = piece.astype(BF16)
                remote(
                    zs_send.at[pos - 1],
                    zs_recv.at[pos - 1],
                    zs_sems.at[0],
                    zs_sems.at[1],
                    z_peer(ORDER[pos]),
                ).start()

    for p in reversed(range(PAIRS)):
        pltpu.make_async_copy(recv2.at[p], recv2.at[p], back_recv.at[p]).wait()
        part = lax.dot_general(
            wmat[p].reshape(384, 256),
            recv2[p].reshape(384, 512),
            (((0,), (0,)), ((), ())),
            preferred_element_type=F32,
        )
        first, second = part[:, 0:256], part[:, 256:512]
        own_part[p] = jnp.where(xl == 0, first, second).reshape(2, 128, 256)
        xs_send[p] = jnp.where(xl == 0, second, first).astype(BF16).reshape(2, 128, 256)
        xs_copy(p).start()
        if p < PAIRS - 1:
            to_owner(p + 1)
    to_owner(0)

    pltpu.make_async_copy(zs_recv, zs_recv, zs_sems.at[1]).wait()
    total = mixed[...] + own_sum[...]
    for d in range(7):
        total = total + zs_recv[d].astype(F32)
    out_ref[...] = total.astype(BF16)

    pltpu.make_async_copy(rs_send, rs_send, rs_sems.at[0]).wait()
    pltpu.make_async_copy(sq_recv, sq_recv, sq_sems.at[0]).wait()
    pltpu.make_async_copy(zs_send, zs_send, zs_sems.at[0]).wait()
    for pos in range(1, NZ):
        hops[pos].wait_send()
    for p in range(PAIRS):
        xs_copy(p).wait_send()
        sent = send1.at[p, pl.ds(0, 7)]
        pltpu.make_async_copy(sent, sent, a2a_send.at[p]).wait()
        sent = recv2.at[p, pl.ds(0, 7)]
        pltpu.make_async_copy(sent, sent, back_send.at[p]).wait()
    for i, (src, dst) in enumerate(weights):
        pltpu.make_async_copy(dst.at[c], dst.at[c], w_send.at[i]).wait()

    @pl.when(swap == 1)
    def _():
        for i, (_, dst) in enumerate(weights):
            pltpu.make_async_copy(dst.at[c], dst.at[c], fwd_send.at[i]).wait()


def shards(
    queries,
    keys,
    values,
    lengths,
    out_weight,
    residual,
    norm_gain,
    expert_ids,
    gate_weights,
    replica_map,
    w_gate,
    w_up,
    w_down,
):
    vmem = pl.BlockSpec(memory_space=pltpu.VMEM)
    hbm = pl.BlockSpec(memory_space=pl.ANY)
    dma = pltpu.SemaphoreType.DMA
    return pl.pallas_call(
        layer_kernel,
        out_shape=jax.ShapeDtypeStruct((128, 256), BF16),
        in_specs=[vmem] * 6 + [hbm] * 7,
        out_specs=vmem,
        scratch_shapes=[
            pltpu.VMEM((4096, 128), BF16),
            pltpu.VMEM((4096, 128), BF16),
            pltpu.VMEM((8, 256, 256), BF16),
            pltpu.VMEM((128, 256), BF16),
            pltpu.VMEM((128, 128), F32),
            pltpu.VMEM((128, 128), F32),
            pltpu.VMEM((2, 64, 256), BF16),
            pltpu.VMEM((2, 64, 256), BF16),
            pltpu.VMEM((7, 128, 256), BF16),
            pltpu.VMEM((7, 128, 256), BF16),
            pltpu.VMEM((128, 256), F32),
            pltpu.VMEM((8, 128), F32),
            pltpu.VMEM((7, 8, 128), F32),
            pltpu.VMEM((2, 128, 256), BF16),
            pltpu.VMEM((8, 16, 128), F32),
            pltpu.VMEM((8, 2, 128, 256), BF16),
            pltpu.VMEM((PAIRS, 8, 2 * CAP, 256), BF16),
            pltpu.VMEM((PAIRS, 8, 2 * CAP, 256), BF16),
            pltpu.VMEM((PAIRS, 8, 2 * CAP, 512), BF16),
            pltpu.VMEM((PAIRS, 4, 2, 2 * CAP, 512), BF16),
            pltpu.VMEM((PAIRS, 4, 2, 2 * CAP, 512), BF16),
            pltpu.VMEM((PAIRS, 8, 2 * CAP, 512), BF16),
            pltpu.VMEM((PAIRS, 2, 128, 256), F32),
            pltpu.VMEM((128, 256), F32),
            pltpu.VMEM((PAIRS, 2, 128, 256), BF16),
            pltpu.VMEM((PAIRS, 2, 128, 256), BF16),
            pltpu.VMEM((7, 128, 256), BF16),
            pltpu.VMEM((7, 128, 256), BF16),
            pltpu.VMEM((2, 192, 2048), BF16),
            pltpu.VMEM((2, 192, 2048), BF16),
            pltpu.VMEM((2, 192, 2048), BF16),
            dma((11,)),
            dma((3,)),
            dma((3,)),
            dma((3,)),
            dma((3,)),
            dma((2,)),
            dma((2,)),
            dma((2,)),
            dma((2,)),
            dma((8,)),
            dma((8,)),
            dma((8,)),
            dma((8,)),
            dma((PAIRS,)),
            dma((PAIRS,)),
            dma((PAIRS,)),
            dma((PAIRS,)),
            dma((PAIRS,)),
            dma((PAIRS,)),
            dma((2,)),
        ],
        compiler_params=pltpu.CompilerParams(
            collective_id=0, has_side_effects=True, vmem_limit_bytes=56 * 2**20
        ),
        name="layer",
    )(
        queries,
        lengths.reshape(1, 128),
        norm_gain.reshape(1, 2048),
        expert_ids.T,
        gate_weights.T,
        replica_map.reshape(1, 128),
        keys.reshape(4096, 128),
        values.reshape(4096, 128),
        out_weight,
        residual,
        w_gate.reshape(2048, 192).T,
        w_up.reshape(2048, 192).T,
        w_down.reshape(192, 2048),
    )


def solution(mesh):
    in_specs = (
        P(("req", "exp"), "kvh"),
        P(("req", "exp"), "kvh", None, None),
        P(("req", "exp"), "kvh", None, None),
        P("req"),
        P(("kvh", "exp"), None),
        P("req", None),
        P(),
        P("req", None),
        P("req", None),
        P(),
        P(("req", "kvh"), None, "exp"),
        P(("req", "kvh"), None, "exp"),
        P(("req", "kvh"), "exp", None),
    )
    out_specs = P("req", ("kvh", "exp"))
    return jax.shard_map(shards, mesh=mesh, in_specs=in_specs, out_specs=out_specs, check_vma=False)
```

```python
import jax
import jax.numpy as jnp
from jax import lax
from jax.experimental import pallas as pl
from jax.experimental.pallas import tpu as pltpu
from jax.sharding import PartitionSpec as P

MESH = pl.DeviceIdType.MESH
F32 = jnp.float32
BF16 = jnp.bfloat16

NZ = 8
CAP = 24
ORDER = (0, 1, 7, 2, 6, 3, 5, 4)
PAIRS = NZ // 2
BLOCKS = (1, 3, 2, 0)


def layer_kernel(
    q_ref,
    len_ref,
    gain_ref,
    ids_ref,
    gates_ref,
    map_ref,
    k_hbm,
    v_hbm,
    ow_hbm,
    res_hbm,
    wg_hbm,
    wu_hbm,
    wd_hbm,
    out_ref,
    kbuf,
    vbuf,
    owb,
    resb,
    lens_t,
    eprim,
    att,
    oh,
    rs_send,
    rs_recv,
    mixed,
    sq_send,
    sq_recv,
    sc,
    rt,
    xg,
    dmat,
    wmat,
    send1,
    recv1,
    send2,
    recv2,
    own_part,
    xs_send,
    xs_recv,
    zs_send,
    zs_recv,
    zx_recv,
    wg,
    wu,
    wd,
    act,
    load_sem,
    w_send,
    w_in,
    fwd_send,
    w_other,
    att_sems,
    rs_send_sem,
    rs_recv_sem,
    sq_sems,
    pair_send,
    pair_recv,
    sc_send,
    sc_recv,
    rt_send,
    rt_recv,
    xg_send,
    xg_recv,
    a2a_send,
    a2a_recv,
    back_send,
    back_recv,
    xs_send_sem,
    xs_recv_sem,
    zs_send_sem,
    zs_recv_sem,
    zx_sems,
):
    req = lax.axis_index("req")
    y = lax.axis_index("kvh")
    xl = lax.axis_index("exp")
    z = lax.div(req, 4)
    xh = lax.rem(lax.div(req, 2), 2)
    c = lax.rem(req, 2)
    blk = y * 2 + xl
    swap = lax.rem(c + xl, 2)

    def serve_peer(d):
        side = d // 4 if isinstance(d, int) else lax.div(d, 4)
        xh_to = lax.rem(xh + side, 2)
        xl_to = lax.rem(xl + side, 2)
        y_to = lax.rem(y + d, 4)
        return side, xh_to, y_to, (z * 4 + xh_to * 2 + c, y_to, xl_to)

    def group_peer(d):
        to = lax.rem(blk + d, 8)
        return to, (req, lax.div(to, 2), lax.rem(to, 2))

    def z_peer(d):
        return (lax.rem(z + d, NZ) * 4 + xh * 2 + c, y, xl)

    exp_peer = (req, y, 1 - xl)
    cross_up = (lax.rem(z + 1, NZ) * 4 + xh * 2 + c, y, 1 - xl)
    cross_down = (lax.rem(z + NZ - 1, NZ) * 4 + xh * 2 + c, y, 1 - xl)
    other_core = (z * 4 + xh * 2 + (1 - c), y, xl)
    swap_peer = (z * 4 + xh * 2 + (1 - c), y, 1 - xl)

    def remote(src, dst, send_sem, recv_sem, device):
        return pltpu.make_async_remote_copy(
            src_ref=src,
            dst_ref=dst,
            send_sem=send_sem,
            recv_sem=recv_sem,
            device_id=device,
            device_id_type=MESH,
        )

    barrier = pltpu.get_barrier_semaphore()

    def greet_group(d, carry):
        pl.semaphore_signal(barrier, inc=1, device_id=group_peer(d)[1], device_id_type=MESH)
        pl.semaphore_signal(barrier, inc=1, device_id=z_peer(d), device_id_type=MESH)
        return carry

    lax.fori_loop(1, 8, greet_group, 0)

    def greet_side(d, carry):
        pl.semaphore_signal(barrier, inc=1, device_id=serve_peer(d)[3], device_id_type=MESH)
        return carry

    lax.fori_loop(4, 8, greet_side, 0)
    for device in (other_core, cross_up, cross_down):
        pl.semaphore_signal(barrier, inc=1, device_id=device, device_id_type=MESH)

    @pl.when(swap == 1)
    def _():
        pl.semaphore_signal(barrier, inc=1, device_id=swap_peer, device_id_type=MESH)

    def load(src, dst, i):
        return pltpu.make_async_copy(src, dst, load_sem.at[i])

    loads = [load(k_hbm, kbuf, 0), load(v_hbm, vbuf, 1)]
    loads.append(
        load(res_hbm.at[:, pl.ds(pl.multiple_of(blk * 256, 256), 256)], resb, 2)
    )
    for b in range(8):
        loads.append(load(ow_hbm.at[:, pl.ds(b * 256, 256)], owb.at[b], 3 + b))
    for one in loads:
        one.start()
    rt[0, 0:8, :] = ids_ref[...].astype(F32)
    rt[0, 8:16, :] = gates_ref[...]
    lens_t[...] = jnp.broadcast_to(len_ref[...].astype(F32), (128, 128)).T

    row = jnp.broadcast_to(map_ref[...].astype(F32), (128, 128))
    col = row.T
    sub = lax.broadcasted_iota(jnp.int32, (128, 128), 0)
    lane = lax.broadcasted_iota(jnp.int32, (128, 128), 1)
    again = jnp.where((row == col) & (lane < sub), 1.0, 0.0)
    eprim[...] = jnp.where(jnp.max(again, axis=1, keepdims=True) > 0.0, -1.0, col)

    loads[0].wait()
    loads[1].wait()
    scale = 128 ** (-0.5)
    rows_at = lax.broadcasted_iota(jnp.int32, (64, 1024), 0)
    cols_at = lax.broadcasted_iota(jnp.int32, (64, 1024), 1)
    same = (rows_at & 15) == (cols_at >> 6)
    at = (cols_at & 63).astype(F32)
    for g in range(4):
        lo = g * 16
        heads = [q_ref[lo : lo + 16, h * 128 : (h + 1) * 128] for h in range(4)]
        q16 = jnp.concatenate(heads, axis=0)
        k16 = kbuf[g * 1024 : (g + 1) * 1024, :]
        s = lax.dot_general(q16, k16, (((1,), (1,)), ((), ())), preferred_element_type=F32)
        own_len = lens_t[pl.ds(pl.multiple_of(xl * 64 + lo, 16), 16), :][:, 0:1]
        live = same & (at < jnp.concatenate([own_len] * 4, axis=0))
        s = jnp.where(live, s * scale, -1e30)
        peak = jnp.max(s, axis=1, keepdims=True)
        w = jnp.where(live, jnp.exp(s - peak), 0.0)
        total = jnp.sum(w, axis=1, keepdims=True)
        v16 = vbuf[g * 1024 : (g + 1) * 1024, :]
        a = jnp.dot(w.astype(BF16), v16, preferred_element_type=F32) / total
        a = a.astype(BF16)
        for h in range(4):
            att[h // 2, lo : lo + 16, (h % 2) * 128 : (h % 2 + 1) * 128] = a[
                h * 16 : (h + 1) * 16, :
            ]
    oh[xl] = att[xl]

    pl.semaphore_wait(barrier, 21 + swap)
    att_copy = remote(att.at[1 - xl], oh.at[xl], att_sems.at[0], att_sems.at[1], exp_peer)
    att_copy.start()

    weights = ((wg_hbm, wg), (wu_hbm, wu))

    def down_columns(k):
        return pl.ds(pl.multiple_of(lax.rem(y + k, 4) * 512, 512), 512)

    def swap_pieces(first, last):
        @pl.when(swap == 1)
        def _():
            for piece in range(first, last):
                if piece < 12:
                    i, part = piece // 6, pl.ds(piece % 6 * 32, 32)
                    src, dst = weights[i]
                    src, dst = src.at[part], dst.at[1 - c, part]
                else:
                    k = BLOCKS[piece - 12]
                    i, src, dst = 2 + k, wd_hbm.at[:, down_columns(k)], wd.at[1 - c, k]
                remote(src, dst, w_send.at[i], w_in.at[i], swap_peer).start()


    @pl.when(swap == 0)
    def _():
        for i, (src, dst) in enumerate(weights):
            pltpu.make_async_copy(src, dst.at[c], w_in.at[i]).start()
            remote(src, dst.at[c], w_send.at[i], w_other.at[i], other_core).start()
        for k in BLOCKS:
            src, dst = wd_hbm.at[:, down_columns(k)], wd.at[c, k]
            pltpu.make_async_copy(src, dst, w_in.at[2 + k]).start()
            remote(src, dst, w_send.at[2 + k], w_other.at[2 + k], other_core).start()

    for pos in range(1, NZ):
        remote(
            rt.at[0], rt.at[pos], rt_send.at[pos], rt_recv.at[pos], z_peer(NZ - ORDER[pos])
        ).start()

    for i in range(2, 11):
        loads[i].wait()
    att_copy.wait()
    heads_all = oh[...].reshape(128, 256)

    def scatter_copy(j, d):
        return remote(
            rs_send.at[j, d - 1],
            rs_recv.at[j, d - 1],
            rs_send_sem.at[j],
            rs_recv_sem.at[j],
            group_peer(d)[1],
        )

    def scatter(d, carry):
        part = jnp.dot(heads_all, owb[group_peer(d)[0]], preferred_element_type=F32)
        part = part.astype(BF16)
        rs_send[0, d - 1] = part[0:64, :]
        scatter_copy(0, d).start()
        rs_send[1, d - 1] = part[64:128, :]
        return carry

    def scatter_rest(d, carry):
        scatter_copy(1, d).start()
        return carry

    lax.fori_loop(1, 8, scatter, 0)
    lax.fori_loop(1, 8, scatter_rest, 0)
    own_out = jnp.dot(heads_all, owb[blk], preferred_element_type=F32)

    for pos in range(1, NZ):
        remote(
            rt.at[0], rt.at[pos], rt_send.at[pos], rt_recv.at[pos], z_peer(NZ - ORDER[pos])
        ).wait()
    first_slot = z * 16 + xh * 8 + xl * 4
    side_slot = z * 16 + (1 - xh) * 8 + (1 - xl) * 4
    expert = jnp.concatenate(
        [eprim[pl.ds(first_slot + i, 1), :] for i in range(4)]
        + [eprim[pl.ds(side_slot + i, 1), :] for i in range(4)],
        axis=0,
    )
    upper = jnp.where(sub < lane, 1.0, 0.0).astype(BF16)
    kk = lax.broadcasted_iota(jnp.int32, (2 * CAP, 256), 0).astype(F32)

    def routing(p, carry):
        places, probs = [], []
        for r in range(2):
            info = rt[2 * p + r]
            ids = info[0:8, :]
            gates = info[8:16, :]
            top = gates / jnp.sum(gates, axis=0, keepdims=True)
            named = jnp.zeros((8, 128), F32)
            prob = jnp.zeros((8, 128), F32)
            for j in range(8):
                hit = ids[j : j + 1, :] == expert
                named = jnp.where(hit, 1.0, named)
                prob = jnp.where(hit, top[j : j + 1, :], prob)
            before = jnp.dot(named.astype(BF16), upper, preferred_element_type=F32)
            places.append(jnp.where(named > 0.0, before + r * CAP, -100.0))
            probs.append(prob)
        place = jnp.concatenate(places, axis=1)
        prob = jnp.concatenate(probs, axis=1)
        for s in range(8):
            chosen = place[s : s + 1, :] == kk
            dmat[p, s] = jnp.where(chosen, 1.0, 0.0).astype(BF16)
            wmat[p, s] = jnp.where(chosen, prob[s : s + 1, :], 0.0).astype(BF16)
        return carry

    lax.fori_loop(0, PAIRS, routing, 0)

    def onward(pos_from, pos_to, step, j):
        return remote(
            xg.at[pos_from, j],
            xg.at[pos_to, j],
            xg_send.at[pos_to, j],
            xg_recv.at[pos_to, j],
            z_peer(step),
        )

    place_of = {offset: pos for pos, offset in enumerate(ORDER)}
    hops = {}
    for j in range(2):
        for k in range(4 - j):
            hops[place_of[k + 1], j] = onward(place_of[k], place_of[k + 1], NZ - 1, j)
        for k in range(3 + j):
            hops[place_of[NZ - 1 - k], j] = onward(
                place_of[(NZ - k) % NZ], place_of[NZ - 1 - k], 1, j
            )

    def share_squares(d, carry):
        remote(
            sq_send, sq_recv.at[d - 1], sq_sems.at[0], sq_sems.at[1], group_peer(d)[1]
        ).start()
        return carry

    def pair_copy(j):
        part = xg.at[0, j, xl]
        return remote(part, part, pair_send.at[j], pair_recv.at[j], exp_peer)

    gain = gain_ref[:, pl.ds(pl.multiple_of(blk * 256, 256), 256)]
    for j in range(2):
        pltpu.make_async_copy(rs_recv.at[j], rs_recv.at[j], rs_recv_sem.at[j]).wait()
        tokens = slice(64 * j, 64 * j + 64)
        total = resb[tokens, :].astype(F32) + own_out[tokens, :]
        for d in range(7):
            total = total + rs_recv[j, d].astype(F32)
        mixed[tokens, :] = total
        xg[0, j, xl] = (total * gain).astype(BF16)
        pair_copy(j).start()
        if j:
            total = mixed[...]
            sq_send[...] = lax.dot_general(
                jnp.ones((8, 256), F32),
                total * total,
                (((1,), (1,)), ((), ())),
                preferred_element_type=F32,
                precision=lax.Precision.HIGHEST,
            )
            lax.fori_loop(1, 8, share_squares, 0)
            swap_pieces(0, 16)
    for j in range(2):
        pair_copy(j).wait_recv()
        hops[1, j].start()
        hops[2, j].start()
    pltpu.make_async_copy(sq_recv, sq_recv, sq_sems.at[1]).wait()
    squares = sq_send[...]
    for d in range(7):
        squares = squares + sq_recv[d]
    sc[0] = lax.rsqrt(squares * (1.0 / 2048.0) + 1e-6)

    def scale_copy(pos):
        return remote(
            sc.at[0], sc.at[pos], sc_send.at[pos], sc_recv.at[pos], z_peer(NZ - ORDER[pos])
        )

    for pos in range(1, NZ):
        scale_copy(pos).start()

    forwards = {
        (1, 0): 3, (2, 0): 4, (1, 1): 3, (2, 1): 4, (3, 0): 5, (4, 0): 6,
        (3, 1): 5, (4, 1): 6, (5, 0): 7, (6, 1): 7,
    }
    for p in range(PAIRS):
        arrive = [pos for pos in (2 * p + 1, 2 * p + 2) if pos < NZ]
        for j in range(2):
            for pos in arrive:
                hops[pos, j].wait_recv()
                if (pos, j) in forwards:
                    hops[forwards[pos, j], j].start()
        scaled = []
        for pos in (2 * p, 2 * p + 1):
            if pos:
                scale_copy(pos).wait_recv()
            factor = jnp.broadcast_to(sc[pos, 0:1, :], (128, 128)).T
            factor = jnp.concatenate([factor, factor], axis=1)
            scaled.append(
                [
                    (xg[pos, :, h].reshape(128, 256).astype(F32) * factor).astype(BF16)
                    for h in range(2)
                ]
            )
        for half in range(2):
            rows = jnp.concatenate([scaled[0][half], scaled[1][half]], axis=0)
            picked = jnp.dot(dmat[p].reshape(384, 256), rows, preferred_element_type=F32)
            send1[p, :, :, half * 256 : (half + 1) * 256] = picked.astype(BF16).reshape(
                8, 2 * CAP, 256
            )

        def dispatch(d, carry, p=p):
            side, _, y_to, device = serve_peer(d)
            remote(
                send1.at[p, side * 4 + y_to],
                recv1.at[p, y, xh],
                a2a_send.at[p],
                a2a_recv.at[p],
                device,
            ).start()
            return carry

        lax.fori_loop(1, 8, dispatch, 0)
        pltpu.make_async_copy(send1.at[p, y], recv1.at[p, y, xh], a2a_recv.at[p]).start()

    def share(i, mine, other):
        pltpu.make_async_copy(mine, mine, w_in.at[i]).wait()

        @pl.when(swap == 1)
        def _():
            remote(mine, mine, fwd_send.at[i], w_other.at[i], other_core).start()

        return pltpu.make_async_copy(other, other, w_other.at[i])

    for one in [share(i, dst.at[c], dst.at[1 - c]) for i, (_, dst) in enumerate(weights)]:
        one.wait()
    contract = (((1,), (1,)), ((), ()))

    def hidden(p):
        pltpu.make_async_copy(recv1.at[p], recv1.at[p], a2a_recv.at[p]).wait()
        rows = jnp.concatenate(
            [recv1[p, b].reshape(4 * CAP, 512) for b in range(4)], axis=1
        )
        for half in range(2):
            gate = lax.dot_general(rows, wg[half], contract, preferred_element_type=F32)
            up = lax.dot_general(rows, wu[half], contract, preferred_element_type=F32)
            act[p, half] = (gate / (1.0 + jnp.exp(-gate)) * up).astype(BF16)

    def down_block(p, k):
        out = jnp.dot(act[p, 0], wd[0, k], preferred_element_type=F32)
        out = out + jnp.dot(act[p, 1], wd[1, k], preferred_element_type=F32)
        send2[p, k] = out.astype(BF16).reshape(2, 2 * CAP, 512)
        for d in (k, 4 + k):
            side, xh_to, _, device = serve_peer(d)
            src, dst = send2.at[p, k, xh_to], recv2.at[p, side * 4 + y]
            if d == 0:
                pltpu.make_async_copy(src, dst, back_recv.at[p]).start()
            else:
                remote(src, dst, back_send.at[p], back_recv.at[p], device).start()

    hidden(0)
    hidden(1)
    hidden(2)
    for k in BLOCKS:
        share(2 + k, wd.at[c, k], wd.at[1 - c, k]).wait()
        down_block(2, k)
    hidden(3)
    for p in (3, 1, 0):
        for k in BLOCKS:
            down_block(p, k)

    def xs_copy(p):
        return remote(
            xs_send.at[p], xs_recv.at[p], xs_send_sem.at[p], xs_recv_sem.at[p], exp_peer
        )

    def combine(p):
        pltpu.make_async_copy(recv2.at[p], recv2.at[p], back_recv.at[p]).wait()
        part = lax.dot_general(
            wmat[p].reshape(384, 256),
            recv2[p].reshape(384, 512),
            (((0,), (0,)), ((), ())),
            preferred_element_type=F32,
        )
        first, second = part[:, 0:256], part[:, 256:512]
        own_part[p] = jnp.where(xl == 0, first, second).reshape(2, 128, 256)
        xs_send[p] = jnp.where(xl == 0, second, first).astype(BF16).reshape(2, 128, 256)

    sent_up = {1: 1, 2: NZ - 1, 3: 2, 4: NZ - 1, 5: 1, 6: NZ - 2, 7: 2}
    added = {2: (4, 6), 3: (5, 7)}

    def z_copy(pos):
        i = pos - 1
        return remote(
            zs_send.at[i],
            zs_recv.at[i],
            zs_send_sem.at[i],
            zs_recv_sem.at[i],
            z_peer(sent_up[pos]),
        )

    def pass_on(pos, cross):
        piece = own_part[pos // 2, pos % 2]
        if cross:
            piece = piece + xs_recv[pos // 2, pos % 2].astype(F32)
        for other in added.get(pos, ()):
            z_copy(other).wait_recv()
            piece = piece + zs_recv[other - 1].astype(F32)
        zs_send[pos - 1] = piece.astype(BF16)
        z_copy(pos).start()

    last_copy = remote(
        xs_send.at[0, 0], xs_recv.at[0, 0], xs_send_sem.at[0], xs_recv_sem.at[0], exp_peer
    )
    cross_copy = remote(xs_send.at[0, 1], zx_recv, zx_sems.at[0], zx_sems.at[1], cross_up)
    combine(2)
    xs_copy(2).start()
    combine(3)
    xs_copy(3).start()
    for p in (2, 3):
        xs_copy(p).wait_recv()
        pass_on(2 * p, True)
        pass_on(2 * p + 1, True)
    combine(1)
    xs_copy(1).start()
    combine(0)
    cross_copy.start()
    last_copy.start()
    pass_on(1, False)
    xs_copy(1).wait_recv()
    pass_on(3, True)
    pass_on(2, True)
    total = mixed[...] + own_part[0, 0]
    last_copy.wait_recv()
    total = total + xs_recv[0, 0].astype(F32)
    cross_copy.wait_recv()
    total = total + zx_recv[...].astype(F32)
    for pos in (1, 2, 3):
        z_copy(pos).wait_recv()
        total = total + zs_recv[pos - 1].astype(F32)
    out_ref[...] = total.astype(BF16)

    for j in range(2):
        pltpu.make_async_copy(rs_send.at[j], rs_send.at[j], rs_send_sem.at[j]).wait()
        pair_copy(j).wait_send()
    pltpu.make_async_copy(sq_recv, sq_recv, sq_sems.at[0]).wait()
    for pos in range(1, NZ):
        z_copy(pos).wait_send()
    last_copy.wait_send()
    cross_copy.wait_send()
    for pos in range(1, NZ):
        hops[pos, 0].wait_send()
        hops[pos, 1].wait_send()
        scale_copy(pos).wait_send()
    for p in range(PAIRS):
        if p:
            xs_copy(p).wait_send()
        sent = send1.at[p, pl.ds(0, 7)]
        pltpu.make_async_copy(sent, sent, a2a_send.at[p]).wait()
        sent = recv2.at[p, pl.ds(0, 7)]
        pltpu.make_async_copy(sent, sent, back_send.at[p]).wait()
    halves = [wg.at[c], wu.at[c]] + [wd.at[c, k] for k in range(4)]
    for i, half in enumerate(halves):
        pltpu.make_async_copy(half, half, w_send.at[i]).wait()

    @pl.when(swap == 1)
    def _():
        for i, half in enumerate(halves):
            pltpu.make_async_copy(half, half, fwd_send.at[i]).wait()


def shards(
    queries,
    keys,
    values,
    lengths,
    out_weight,
    residual,
    norm_gain,
    expert_ids,
    gate_weights,
    replica_map,
    w_gate,
    w_up,
    w_down,
):
    vmem = pl.BlockSpec(memory_space=pltpu.VMEM)
    hbm = pl.BlockSpec(memory_space=pl.ANY)
    dma = pltpu.SemaphoreType.DMA
    return pl.pallas_call(
        layer_kernel,
        out_shape=jax.ShapeDtypeStruct((128, 256), BF16),
        in_specs=[vmem] * 6 + [hbm] * 7,
        out_specs=vmem,
        scratch_shapes=[
            pltpu.VMEM((4096, 128), BF16),
            pltpu.VMEM((4096, 128), BF16),
            pltpu.VMEM((8, 256, 256), BF16),
            pltpu.VMEM((128, 256), BF16),
            pltpu.VMEM((128, 128), F32),
            pltpu.VMEM((128, 128), F32),
            pltpu.VMEM((2, 64, 256), BF16),
            pltpu.VMEM((2, 64, 256), BF16),
            pltpu.VMEM((2, 7, 64, 256), BF16),
            pltpu.VMEM((2, 7, 64, 256), BF16),
            pltpu.VMEM((128, 256), F32),
            pltpu.VMEM((8, 128), F32),
            pltpu.VMEM((7, 8, 128), F32),
            pltpu.VMEM((8, 8, 128), F32),
            pltpu.VMEM((8, 16, 128), F32),
            pltpu.VMEM((8, 2, 2, 64, 256), BF16),
            pltpu.VMEM((PAIRS, 8, 2 * CAP, 256), BF16),
            pltpu.VMEM((PAIRS, 8, 2 * CAP, 256), BF16),
            pltpu.VMEM((PAIRS, 8, 2 * CAP, 512), BF16),
            pltpu.VMEM((PAIRS, 4, 2, 2 * CAP, 512), BF16),
            pltpu.VMEM((PAIRS, 4, 2, 2 * CAP, 512), BF16),
            pltpu.VMEM((PAIRS, 8, 2 * CAP, 512), BF16),
            pltpu.VMEM((PAIRS, 2, 128, 256), F32),
            pltpu.VMEM((PAIRS, 2, 128, 256), BF16),
            pltpu.VMEM((PAIRS, 2, 128, 256), BF16),
            pltpu.VMEM((7, 128, 256), BF16),
            pltpu.VMEM((7, 128, 256), BF16),
            pltpu.VMEM((128, 256), BF16),
            pltpu.VMEM((2, 192, 2048), BF16),
            pltpu.VMEM((2, 192, 2048), BF16),
            pltpu.VMEM((2, 4, 192, 512), BF16),
            pltpu.VMEM((PAIRS, 2, 4 * CAP, 192), BF16),
            dma((11,)),
            dma((6,)),
            dma((6,)),
            dma((6,)),
            dma((6,)),
            dma((2,)),
            dma((2,)),
            dma((2,)),
            dma((2,)),
            dma((2,)),
            dma((2,)),
            dma((8,)),
            dma((8,)),
            dma((8,)),
            dma((8,)),
            dma((8, 2)),
            dma((8, 2)),
            dma((PAIRS,)),
            dma((PAIRS,)),
            dma((PAIRS,)),
            dma((PAIRS,)),
            dma((PAIRS,)),
            dma((PAIRS,)),
            dma((7,)),
            dma((7,)),
            dma((2,)),
        ],
        compiler_params=pltpu.CompilerParams(
            collective_id=0, has_side_effects=True, vmem_limit_bytes=56 * 2**20
        ),
        name="layer",
    )(
        queries,
        lengths.reshape(1, 128),
        norm_gain.reshape(1, 2048),
        expert_ids.T,
        gate_weights.T,
        replica_map.reshape(1, 128),
        keys.reshape(4096, 128),
        values.reshape(4096, 128),
        out_weight,
        residual,
        w_gate.reshape(2048, 192).T,
        w_up.reshape(2048, 192).T,
        w_down.reshape(192, 2048),
    )


def solution(mesh):
    in_specs = (
        P(("req", "exp"), "kvh"),
        P(("req", "exp"), "kvh", None, None),
        P(("req", "exp"), "kvh", None, None),
        P("req"),
        P(("kvh", "exp"), None),
        P("req", None),
        P(),
        P("req", None),
        P("req", None),
        P(),
        P(("req", "kvh"), None, "exp"),
        P(("req", "kvh"), None, "exp"),
        P(("req", "kvh"), "exp", None),
    )
    out_specs = P("req", ("kvh", "exp"))
    return jax.shard_map(shards, mesh=mesh, in_specs=in_specs, out_specs=out_specs, check_vma=False)
```

```python
import jax
import jax.numpy as jnp
from jax import lax
from jax.experimental import pallas as pl
from jax.experimental.pallas import tpu as pltpu
from jax.sharding import PartitionSpec as P

MESH = pl.DeviceIdType.MESH
F32 = jnp.float32
BF16 = jnp.bfloat16

NZ = 8
CAP = 24
ORDER = (0, 1, 7, 2, 6, 3, 5, 4)
PAIRS = NZ // 2
BLOCKS = (1, 3, 2, 0)


def layer_kernel(
    q_ref,
    len_ref,
    gain_ref,
    ids_ref,
    gates_ref,
    map_ref,
    k_hbm,
    v_hbm,
    ow_hbm,
    res_hbm,
    wg_hbm,
    wu_hbm,
    wd_hbm,
    out_ref,
    kbuf,
    vbuf,
    owb,
    resb,
    lens_t,
    eprim,
    att,
    oh,
    rs_send,
    rs_recv,
    mixed,
    sq_send,
    sq_recv,
    sc,
    rt,
    xg,
    dmat,
    wmat,
    send1,
    recv1,
    send2,
    recv2,
    own_part,
    xs_send,
    xs_recv,
    zs_send,
    zs_recv,
    zx_recv,
    wg,
    wu,
    wd,
    act,
    load_sem,
    w_send,
    w_in,
    fwd_send,
    w_other,
    att_sems,
    rs_send_sem,
    rs_recv_sem,
    sq_sems,
    pair_send,
    pair_recv,
    sc_send,
    sc_recv,
    rt_send,
    rt_recv,
    xg_send,
    xg_recv,
    a2a_send,
    a2a_recv,
    back_send,
    back_recv,
    xs_send_sem,
    xs_recv_sem,
    zs_send_sem,
    zs_recv_sem,
    zx_sems,
):
    req = lax.axis_index("req")
    y = lax.axis_index("kvh")
    xl = lax.axis_index("exp")
    z = lax.div(req, 4)
    xh = lax.rem(lax.div(req, 2), 2)
    c = lax.rem(req, 2)
    blk = y * 2 + xl
    swap = lax.rem(c + xl, 2)

    def serve_peer(d):
        side = d // 4 if isinstance(d, int) else lax.div(d, 4)
        xh_to = lax.rem(xh + side, 2)
        xl_to = lax.rem(xl + side, 2)
        y_to = lax.rem(y + d, 4)
        return side, xh_to, y_to, (z * 4 + xh_to * 2 + c, y_to, xl_to)

    def group_peer(d):
        to = lax.rem(blk + d, 8)
        return to, (req, lax.div(to, 2), lax.rem(to, 2))

    def z_peer(d):
        return (lax.rem(z + d, NZ) * 4 + xh * 2 + c, y, xl)

    exp_peer = (req, y, 1 - xl)
    cross_up = (lax.rem(z + 1, NZ) * 4 + xh * 2 + c, y, 1 - xl)
    cross_down = (lax.rem(z + NZ - 1, NZ) * 4 + xh * 2 + c, y, 1 - xl)
    other_core = (z * 4 + xh * 2 + (1 - c), y, xl)
    swap_peer = (z * 4 + xh * 2 + (1 - c), y, 1 - xl)

    def remote(src, dst, send_sem, recv_sem, device):
        return pltpu.make_async_remote_copy(
            src_ref=src,
            dst_ref=dst,
            send_sem=send_sem,
            recv_sem=recv_sem,
            device_id=device,
            device_id_type=MESH,
        )

    barrier = pltpu.get_barrier_semaphore()

    def greet_group(d, carry):
        pl.semaphore_signal(barrier, inc=1, device_id=group_peer(d)[1], device_id_type=MESH)
        pl.semaphore_signal(barrier, inc=1, device_id=z_peer(d), device_id_type=MESH)
        return carry

    lax.fori_loop(1, 8, greet_group, 0)

    def greet_side(d, carry):
        pl.semaphore_signal(barrier, inc=1, device_id=serve_peer(d)[3], device_id_type=MESH)
        return carry

    lax.fori_loop(4, 8, greet_side, 0)
    for device in (other_core, cross_up, cross_down):
        pl.semaphore_signal(barrier, inc=1, device_id=device, device_id_type=MESH)

    @pl.when(swap == 1)
    def _():
        pl.semaphore_signal(barrier, inc=1, device_id=swap_peer, device_id_type=MESH)

    def load(src, dst, i):
        return pltpu.make_async_copy(src, dst, load_sem.at[i])

    loads = [load(k_hbm, kbuf, 0), load(v_hbm, vbuf, 1)]
    loads.append(
        load(res_hbm.at[:, pl.ds(pl.multiple_of(blk * 256, 256), 256)], resb, 2)
    )
    for b in range(8):
        loads.append(load(ow_hbm.at[:, pl.ds(b * 256, 256)], owb.at[b], 3 + b))
    for one in loads:
        one.start()
    rt[0, 0:8, :] = ids_ref[...].astype(F32)
    rt[0, 8:16, :] = gates_ref[...]
    lens_t[...] = jnp.broadcast_to(len_ref[...].astype(F32), (128, 128)).T

    row = jnp.broadcast_to(map_ref[...].astype(F32), (128, 128))
    col = row.T
    sub = lax.broadcasted_iota(jnp.int32, (128, 128), 0)
    lane = lax.broadcasted_iota(jnp.int32, (128, 128), 1)
    again = jnp.where((row == col) & (lane < sub), 1.0, 0.0)
    eprim[...] = jnp.where(jnp.max(again, axis=1, keepdims=True) > 0.0, -1.0, col)

    loads[0].wait()
    loads[1].wait()
    scale = 128 ** (-0.5)
    rows_at = lax.broadcasted_iota(jnp.int32, (64, 1024), 0)
    cols_at = lax.broadcasted_iota(jnp.int32, (64, 1024), 1)
    same = (rows_at & 15) == (cols_at >> 6)
    at = (cols_at & 63).astype(F32)
    for g in range(4):
        lo = g * 16
        heads = [q_ref[lo : lo + 16, h * 128 : (h + 1) * 128] for h in range(4)]
        q16 = jnp.concatenate(heads, axis=0)
        k16 = kbuf[g * 1024 : (g + 1) * 1024, :]
        s = lax.dot_general(q16, k16, (((1,), (1,)), ((), ())), preferred_element_type=F32)
        own_len = lens_t[pl.ds(pl.multiple_of(xl * 64 + lo, 16), 16), :][:, 0:1]
        live = same & (at < jnp.concatenate([own_len] * 4, axis=0))
        s = jnp.where(live, s * scale, -1e30)
        peak = jnp.max(s, axis=1, keepdims=True)
        w = jnp.where(live, jnp.exp(s - peak), 0.0)
        total = jnp.sum(w, axis=1, keepdims=True)
        v16 = vbuf[g * 1024 : (g + 1) * 1024, :]
        a = jnp.dot(w.astype(BF16), v16, preferred_element_type=F32) / total
        a = a.astype(BF16)
        for h in range(4):
            att[h // 2, lo : lo + 16, (h % 2) * 128 : (h % 2 + 1) * 128] = a[
                h * 16 : (h + 1) * 16, :
            ]
    oh[xl] = att[xl]

    pl.semaphore_wait(barrier, 21 + swap)
    att_copy = remote(att.at[1 - xl], oh.at[xl], att_sems.at[0], att_sems.at[1], exp_peer)
    att_copy.start()

    weights = ((wg_hbm, wg), (wu_hbm, wu))

    def down_columns(k):
        return pl.ds(pl.multiple_of(lax.rem(y + k, 4) * 512, 512), 512)

    def swap_pieces(first, last):
        @pl.when(swap == 1)
        def _():
            for piece in range(first, last):
                if piece < 2:
                    i = piece
                    src, dst = weights[i][0], weights[i][1].at[1 - c]
                else:
                    k = BLOCKS[piece - 2]
                    i, src, dst = 2 + k, wd_hbm.at[:, down_columns(k)], wd.at[1 - c, k]
                remote(src, dst, w_send.at[i], w_in.at[i], swap_peer).start()


    @pl.when(swap == 0)
    def _():
        for i, (src, dst) in enumerate(weights):
            pltpu.make_async_copy(src, dst.at[c], w_in.at[i]).start()
            remote(src, dst.at[c], w_send.at[i], w_other.at[i], other_core).start()
        for k in BLOCKS:
            src, dst = wd_hbm.at[:, down_columns(k)], wd.at[c, k]
            pltpu.make_async_copy(src, dst, w_in.at[2 + k]).start()
            remote(src, dst, w_send.at[2 + k], w_other.at[2 + k], other_core).start()

    for pos in range(1, NZ):
        remote(
            rt.at[0], rt.at[pos], rt_send.at[pos], rt_recv.at[pos], z_peer(NZ - ORDER[pos])
        ).start()

    for i in range(2, 11):
        loads[i].wait()
    att_copy.wait()
    heads_all = oh[...].reshape(128, 256)

    def scatter_copy(j, d):
        return remote(
            rs_send.at[j, d - 1],
            rs_recv.at[j, d - 1],
            rs_send_sem.at[j],
            rs_recv_sem.at[j],
            group_peer(d)[1],
        )

    def scatter(d, carry):
        part = jnp.dot(heads_all, owb[group_peer(d)[0]], preferred_element_type=F32)
        part = part.astype(BF16)
        rs_send[0, d - 1] = part[0:64, :]
        scatter_copy(0, d).start()
        rs_send[1, d - 1] = part[64:128, :]
        return carry

    def scatter_rest(d, carry):
        scatter_copy(1, d).start()
        return carry

    lax.fori_loop(1, 8, scatter, 0)
    lax.fori_loop(1, 8, scatter_rest, 0)
    own_out = jnp.dot(heads_all, owb[blk], preferred_element_type=F32)

    for pos in range(1, NZ):
        remote(
            rt.at[0], rt.at[pos], rt_send.at[pos], rt_recv.at[pos], z_peer(NZ - ORDER[pos])
        ).wait()
    first_slot = z * 16 + xh * 8 + xl * 4
    side_slot = z * 16 + (1 - xh) * 8 + (1 - xl) * 4
    expert = jnp.concatenate(
        [eprim[pl.ds(first_slot + i, 1), :] for i in range(4)]
        + [eprim[pl.ds(side_slot + i, 1), :] for i in range(4)],
        axis=0,
    )
    upper = jnp.where(sub < lane, 1.0, 0.0).astype(BF16)
    kk = lax.broadcasted_iota(jnp.int32, (2 * CAP, 256), 0).astype(F32)

    def routing(p, carry):
        places, probs = [], []
        for r in range(2):
            info = rt[2 * p + r]
            ids = info[0:8, :]
            gates = info[8:16, :]
            top = gates / jnp.sum(gates, axis=0, keepdims=True)
            named = jnp.zeros((8, 128), F32)
            prob = jnp.zeros((8, 128), F32)
            for j in range(8):
                hit = ids[j : j + 1, :] == expert
                named = jnp.where(hit, 1.0, named)
                prob = jnp.where(hit, top[j : j + 1, :], prob)
            before = jnp.dot(named.astype(BF16), upper, preferred_element_type=F32)
            places.append(jnp.where(named > 0.0, before + r * CAP, -100.0))
            probs.append(prob)
        place = jnp.concatenate(places, axis=1)
        prob = jnp.concatenate(probs, axis=1)
        for s in range(8):
            chosen = place[s : s + 1, :] == kk
            dmat[p, s] = jnp.where(chosen, 1.0, 0.0).astype(BF16)
            wmat[p, s] = jnp.where(chosen, prob[s : s + 1, :], 0.0).astype(BF16)
        return carry

    lax.fori_loop(0, PAIRS, routing, 0)

    def onward(pos_from, pos_to, step, j):
        return remote(
            xg.at[pos_from, j],
            xg.at[pos_to, j],
            xg_send.at[pos_to, j],
            xg_recv.at[pos_to, j],
            z_peer(step),
        )

    place_of = {offset: pos for pos, offset in enumerate(ORDER)}
    hops = {}
    for j in range(2):
        for k in range(4 - j):
            hops[place_of[k + 1], j] = onward(place_of[k], place_of[k + 1], NZ - 1, j)
        for k in range(3 + j):
            hops[place_of[NZ - 1 - k], j] = onward(
                place_of[(NZ - k) % NZ], place_of[NZ - 1 - k], 1, j
            )

    def share_squares(d, carry):
        remote(
            sq_send, sq_recv.at[d - 1], sq_sems.at[0], sq_sems.at[1], group_peer(d)[1]
        ).start()
        return carry

    def pair_copy(j):
        part = xg.at[0, j, xl]
        return remote(part, part, pair_send.at[j], pair_recv.at[j], exp_peer)

    gain = gain_ref[:, pl.ds(pl.multiple_of(blk * 256, 256), 256)]
    for j in range(2):
        pltpu.make_async_copy(rs_recv.at[j], rs_recv.at[j], rs_recv_sem.at[j]).wait()
        tokens = slice(64 * j, 64 * j + 64)
        total = resb[tokens, :].astype(F32) + own_out[tokens, :]
        for d in range(7):
            total = total + rs_recv[j, d].astype(F32)
        mixed[tokens, :] = total
        xg[0, j, xl] = (total * gain).astype(BF16)
        pair_copy(j).start()
        if j:
            total = mixed[...]
            sq_send[...] = lax.dot_general(
                jnp.ones((8, 256), F32),
                total * total,
                (((1,), (1,)), ((), ())),
                preferred_element_type=F32,
                precision=lax.Precision.HIGHEST,
            )
            lax.fori_loop(1, 8, share_squares, 0)
            swap_pieces(0, 6)
    for j in range(2):
        pair_copy(j).wait_recv()
        hops[1, j].start()
        hops[2, j].start()
    pltpu.make_async_copy(sq_recv, sq_recv, sq_sems.at[1]).wait()
    squares = sq_send[...]
    for d in range(7):
        squares = squares + sq_recv[d]
    sc[0] = lax.rsqrt(squares * (1.0 / 2048.0) + 1e-6)

    def scale_copy(pos):
        return remote(
            sc.at[0], sc.at[pos], sc_send.at[pos], sc_recv.at[pos], z_peer(NZ - ORDER[pos])
        )

    for pos in range(1, NZ):
        scale_copy(pos).start()

    forwards = {
        (1, 0): 3, (2, 0): 4, (1, 1): 3, (2, 1): 4, (3, 0): 5, (4, 0): 6,
        (3, 1): 5, (4, 1): 6, (5, 0): 7, (6, 1): 7,
    }
    for p in range(PAIRS):
        arrive = [pos for pos in (2 * p + 1, 2 * p + 2) if pos < NZ]
        for j in range(2):
            for pos in arrive:
                hops[pos, j].wait_recv()
                if (pos, j) in forwards:
                    hops[forwards[pos, j], j].start()
        scaled = []
        for pos in (2 * p, 2 * p + 1):
            if pos:
                scale_copy(pos).wait_recv()
            factor = jnp.broadcast_to(sc[pos, 0:1, :], (128, 128)).T
            factor = jnp.concatenate([factor, factor], axis=1)
            scaled.append(
                [
                    (xg[pos, :, h].reshape(128, 256).astype(F32) * factor).astype(BF16)
                    for h in range(2)
                ]
            )
        for half in range(2):
            rows = jnp.concatenate([scaled[0][half], scaled[1][half]], axis=0)
            picked = jnp.dot(dmat[p].reshape(384, 256), rows, preferred_element_type=F32)
            send1[p, :, :, half * 256 : (half + 1) * 256] = picked.astype(BF16).reshape(
                8, 2 * CAP, 256
            )

        def dispatch(d, carry, p=p):
            side, _, y_to, device = serve_peer(d)
            remote(
                send1.at[p, side * 4 + y_to],
                recv1.at[p, y, xh],
                a2a_send.at[p],
                a2a_recv.at[p],
                device,
            ).start()
            return carry

        lax.fori_loop(1, 8, dispatch, 0)
        pltpu.make_async_copy(send1.at[p, y], recv1.at[p, y, xh], a2a_recv.at[p]).start()

    def share(i, mine, other):
        pltpu.make_async_copy(mine, mine, w_in.at[i]).wait()

        @pl.when(swap == 1)
        def _():
            remote(mine, mine, fwd_send.at[i], w_other.at[i], other_core).start()

        return pltpu.make_async_copy(other, other, w_other.at[i])

    for one in [share(i, dst.at[c], dst.at[1 - c]) for i, (_, dst) in enumerate(weights)]:
        one.wait()
    contract = (((1,), (1,)), ((), ()))

    def hidden(p):
        pltpu.make_async_copy(recv1.at[p], recv1.at[p], a2a_recv.at[p]).wait()
        rows = jnp.concatenate(
            [recv1[p, b].reshape(4 * CAP, 512) for b in range(4)], axis=1
        )
        for half in range(2):
            gate = lax.dot_general(rows, wg[half], contract, preferred_element_type=F32)
            up = lax.dot_general(rows, wu[half], contract, preferred_element_type=F32)
            act[p, half] = (gate / (1.0 + jnp.exp(-gate)) * up).astype(BF16)

    def down_block(p, k):
        out = jnp.dot(act[p, 0], wd[0, k], preferred_element_type=F32)
        out = out + jnp.dot(act[p, 1], wd[1, k], preferred_element_type=F32)
        send2[p, k] = out.astype(BF16).reshape(2, 2 * CAP, 512)
        for d in (k, 4 + k):
            side, xh_to, _, device = serve_peer(d)
            src, dst = send2.at[p, k, xh_to], recv2.at[p, side * 4 + y]
            if d == 0:
                pltpu.make_async_copy(src, dst, back_recv.at[p]).start()
            else:
                remote(src, dst, back_send.at[p], back_recv.at[p], device).start()

    hidden(0)
    hidden(1)
    hidden(2)
    for k in BLOCKS:
        share(2 + k, wd.at[c, k], wd.at[1 - c, k]).wait()
        down_block(2, k)
    hidden(3)
    for p in (3, 1, 0):
        for k in BLOCKS:
            down_block(p, k)

    def xs_copy(p):
        return remote(
            xs_send.at[p], xs_recv.at[p], xs_send_sem.at[p], xs_recv_sem.at[p], exp_peer
        )

    def combine(p):
        pltpu.make_async_copy(recv2.at[p], recv2.at[p], back_recv.at[p]).wait()
        part = lax.dot_general(
            wmat[p].reshape(384, 256),
            recv2[p].reshape(384, 512),
            (((0,), (0,)), ((), ())),
            preferred_element_type=F32,
        )
        first, second = part[:, 0:256], part[:, 256:512]
        own_part[p] = jnp.where(xl == 0, first, second).reshape(2, 128, 256)
        xs_send[p] = jnp.where(xl == 0, second, first).astype(BF16).reshape(2, 128, 256)

    sent_up = {1: 1, 2: NZ - 1, 3: 2, 4: NZ - 1, 5: 1, 6: NZ - 2, 7: 2}
    added = {2: (4, 6), 3: (5, 7)}

    def z_copy(pos):
        i = pos - 1
        return remote(
            zs_send.at[i],
            zs_recv.at[i],
            zs_send_sem.at[i],
            zs_recv_sem.at[i],
            z_peer(sent_up[pos]),
        )

    def pass_on(pos, cross):
        piece = own_part[pos // 2, pos % 2]
        if cross:
            piece = piece + xs_recv[pos // 2, pos % 2].astype(F32)
        for other in added.get(pos, ()):
            z_copy(other).wait_recv()
            piece = piece + zs_recv[other - 1].astype(F32)
        zs_send[pos - 1] = piece.astype(BF16)
        z_copy(pos).start()

    last_copy = remote(
        xs_send.at[0, 0], xs_recv.at[0, 0], xs_send_sem.at[0], xs_recv_sem.at[0], exp_peer
    )
    cross_copy = remote(xs_send.at[0, 1], zx_recv, zx_sems.at[0], zx_sems.at[1], cross_up)
    combine(2)
    xs_copy(2).start()
    combine(3)
    xs_copy(3).start()
    for p in (2, 3):
        xs_copy(p).wait_recv()
        pass_on(2 * p, True)
        pass_on(2 * p + 1, True)
    combine(1)
    xs_copy(1).start()
    combine(0)
    last_copy.start()
    pass_on(1, False)
    cross_copy.start()
    xs_copy(1).wait_recv()
    pass_on(3, True)
    pass_on(2, True)
    total = mixed[...] + own_part[0, 0]
    last_copy.wait_recv()
    total = total + xs_recv[0, 0].astype(F32)
    cross_copy.wait_recv()
    total = total + zx_recv[...].astype(F32)
    for pos in (1, 2, 3):
        z_copy(pos).wait_recv()
        total = total + zs_recv[pos - 1].astype(F32)
    out_ref[...] = total.astype(BF16)

    for j in range(2):
        pltpu.make_async_copy(rs_send.at[j], rs_send.at[j], rs_send_sem.at[j]).wait()
        pair_copy(j).wait_send()
    pltpu.make_async_copy(sq_recv, sq_recv, sq_sems.at[0]).wait()
    for pos in range(1, NZ):
        z_copy(pos).wait_send()
    last_copy.wait_send()
    cross_copy.wait_send()
    for pos in range(1, NZ):
        hops[pos, 0].wait_send()
        hops[pos, 1].wait_send()
        scale_copy(pos).wait_send()
    for p in range(PAIRS):
        if p:
            xs_copy(p).wait_send()
        sent = send1.at[p, pl.ds(0, 7)]
        pltpu.make_async_copy(sent, sent, a2a_send.at[p]).wait()
        sent = recv2.at[p, pl.ds(0, 7)]
        pltpu.make_async_copy(sent, sent, back_send.at[p]).wait()
    halves = [wg.at[c], wu.at[c]] + [wd.at[c, k] for k in range(4)]
    for i, half in enumerate(halves):
        pltpu.make_async_copy(half, half, w_send.at[i]).wait()

    @pl.when(swap == 1)
    def _():
        for i, half in enumerate(halves):
            pltpu.make_async_copy(half, half, fwd_send.at[i]).wait()


def shards(
    queries,
    keys,
    values,
    lengths,
    out_weight,
    residual,
    norm_gain,
    expert_ids,
    gate_weights,
    replica_map,
    w_gate,
    w_up,
    w_down,
):
    vmem = pl.BlockSpec(memory_space=pltpu.VMEM)
    hbm = pl.BlockSpec(memory_space=pl.ANY)
    dma = pltpu.SemaphoreType.DMA
    return pl.pallas_call(
        layer_kernel,
        out_shape=jax.ShapeDtypeStruct((128, 256), BF16),
        in_specs=[vmem] * 6 + [hbm] * 7,
        out_specs=vmem,
        scratch_shapes=[
            pltpu.VMEM((4096, 128), BF16),
            pltpu.VMEM((4096, 128), BF16),
            pltpu.VMEM((8, 256, 256), BF16),
            pltpu.VMEM((128, 256), BF16),
            pltpu.VMEM((128, 128), F32),
            pltpu.VMEM((128, 128), F32),
            pltpu.VMEM((2, 64, 256), BF16),
            pltpu.VMEM((2, 64, 256), BF16),
            pltpu.VMEM((2, 7, 64, 256), BF16),
            pltpu.VMEM((2, 7, 64, 256), BF16),
            pltpu.VMEM((128, 256), F32),
            pltpu.VMEM((8, 128), F32),
            pltpu.VMEM((7, 8, 128), F32),
            pltpu.VMEM((8, 8, 128), F32),
            pltpu.VMEM((8, 16, 128), F32),
            pltpu.VMEM((8, 2, 2, 64, 256), BF16),
            pltpu.VMEM((PAIRS, 8, 2 * CAP, 256), BF16),
            pltpu.VMEM((PAIRS, 8, 2 * CAP, 256), BF16),
            pltpu.VMEM((PAIRS, 8, 2 * CAP, 512), BF16),
            pltpu.VMEM((PAIRS, 4, 2, 2 * CAP, 512), BF16),
            pltpu.VMEM((PAIRS, 4, 2, 2 * CAP, 512), BF16),
            pltpu.VMEM((PAIRS, 8, 2 * CAP, 512), BF16),
            pltpu.VMEM((PAIRS, 2, 128, 256), F32),
            pltpu.VMEM((PAIRS, 2, 128, 256), BF16),
            pltpu.VMEM((PAIRS, 2, 128, 256), BF16),
            pltpu.VMEM((7, 128, 256), BF16),
            pltpu.VMEM((7, 128, 256), BF16),
            pltpu.VMEM((128, 256), BF16),
            pltpu.VMEM((2, 192, 2048), BF16),
            pltpu.VMEM((2, 192, 2048), BF16),
            pltpu.VMEM((2, 4, 192, 512), BF16),
            pltpu.VMEM((PAIRS, 2, 4 * CAP, 192), BF16),
            dma((11,)),
            dma((6,)),
            dma((6,)),
            dma((6,)),
            dma((6,)),
            dma((2,)),
            dma((2,)),
            dma((2,)),
            dma((2,)),
            dma((2,)),
            dma((2,)),
            dma((8,)),
            dma((8,)),
            dma((8,)),
            dma((8,)),
            dma((8, 2)),
            dma((8, 2)),
            dma((PAIRS,)),
            dma((PAIRS,)),
            dma((PAIRS,)),
            dma((PAIRS,)),
            dma((PAIRS,)),
            dma((PAIRS,)),
            dma((7,)),
            dma((7,)),
            dma((2,)),
        ],
        compiler_params=pltpu.CompilerParams(
            collective_id=0, has_side_effects=True, vmem_limit_bytes=56 * 2**20
        ),
        name="layer",
    )(
        queries,
        lengths.reshape(1, 128),
        norm_gain.reshape(1, 2048),
        expert_ids.T,
        gate_weights.T,
        replica_map.reshape(1, 128),
        keys.reshape(4096, 128),
        values.reshape(4096, 128),
        out_weight,
        residual,
        w_gate.reshape(2048, 192).T,
        w_up.reshape(2048, 192).T,
        w_down.reshape(192, 2048),
    )


def solution(mesh):
    in_specs = (
        P(("req", "exp"), "kvh"),
        P(("req", "exp"), "kvh", None, None),
        P(("req", "exp"), "kvh", None, None),
        P("req"),
        P(("kvh", "exp"), None),
        P("req", None),
        P(),
        P("req", None),
        P("req", None),
        P(),
        P(("req", "kvh"), None, "exp"),
        P(("req", "kvh"), None, "exp"),
        P(("req", "kvh"), "exp", None),
    )
    out_specs = P("req", ("kvh", "exp"))
    return jax.shard_map(shards, mesh=mesh, in_specs=in_specs, out_specs=out_specs, check_vma=False)
```

```python
import jax
import jax.numpy as jnp
from jax import lax
from jax.experimental import pallas as pl
from jax.experimental.pallas import tpu as pltpu
from jax.sharding import PartitionSpec as P

MESH = pl.DeviceIdType.MESH
F32 = jnp.float32
BF16 = jnp.bfloat16

NZ = 8
CAP = 24
ORDER = (0, 1, 7, 2, 6, 3, 5, 4)
PAIRS = NZ // 2
BLOCKS = (1, 3, 2, 0)


def layer_kernel(
    q_ref,
    len_ref,
    gain_ref,
    ids_ref,
    gates_ref,
    map_ref,
    k_hbm,
    v_hbm,
    ow_hbm,
    res_hbm,
    wg_hbm,
    wu_hbm,
    wd_hbm,
    out_ref,
    kbuf,
    vbuf,
    owb,
    resb,
    lens_t,
    eprim,
    att,
    oh,
    rs_send,
    rs_recv,
    mixed,
    sq_send,
    sq_recv,
    sc,
    rt,
    xg,
    dmat,
    wmat,
    send1,
    recv1,
    send2,
    recv2,
    own_part,
    xs_send,
    xs_recv,
    zs_send,
    zs_recv,
    zx_recv,
    wg,
    wu,
    wd,
    act,
    load_sem,
    w_send,
    w_in,
    fwd_send,
    w_other,
    att_sems,
    rs_send_sem,
    rs_recv_sem,
    sq_sems,
    pair_send,
    pair_recv,
    sc_send,
    sc_recv,
    rt_send,
    rt_recv,
    xg_send,
    xg_recv,
    a2a_send,
    a2a_recv,
    back_send,
    back_recv,
    xs_send_sem,
    xs_recv_sem,
    zs_send_sem,
    zs_recv_sem,
    zx_sems,
):
    req = lax.axis_index("req")
    y = lax.axis_index("kvh")
    xl = lax.axis_index("exp")
    z = lax.div(req, 4)
    xh = lax.rem(lax.div(req, 2), 2)
    c = lax.rem(req, 2)
    blk = y * 2 + xl
    swap = lax.rem(c + xl, 2)

    def serve_peer(d):
        side = d // 4 if isinstance(d, int) else lax.div(d, 4)
        xh_to = lax.rem(xh + side, 2)
        xl_to = lax.rem(xl + side, 2)
        y_to = lax.rem(y + d, 4)
        return side, xh_to, y_to, (z * 4 + xh_to * 2 + c, y_to, xl_to)

    def group_peer(d):
        to = lax.rem(blk + d, 8)
        return to, (req, lax.div(to, 2), lax.rem(to, 2))

    def z_peer(d):
        return (lax.rem(z + d, NZ) * 4 + xh * 2 + c, y, xl)

    exp_peer = (req, y, 1 - xl)
    cross_up = (lax.rem(z + 1, NZ) * 4 + xh * 2 + c, y, 1 - xl)
    cross_down = (lax.rem(z + NZ - 1, NZ) * 4 + xh * 2 + c, y, 1 - xl)
    other_core = (z * 4 + xh * 2 + (1 - c), y, xl)
    swap_peer = (z * 4 + xh * 2 + (1 - c), y, 1 - xl)

    def remote(src, dst, send_sem, recv_sem, device):
        return pltpu.make_async_remote_copy(
            src_ref=src,
            dst_ref=dst,
            send_sem=send_sem,
            recv_sem=recv_sem,
            device_id=device,
            device_id_type=MESH,
        )

    barrier = pltpu.get_barrier_semaphore()

    def greet_group(d, carry):
        pl.semaphore_signal(barrier, inc=1, device_id=group_peer(d)[1], device_id_type=MESH)
        pl.semaphore_signal(barrier, inc=1, device_id=z_peer(d), device_id_type=MESH)
        return carry

    lax.fori_loop(1, 8, greet_group, 0)

    def greet_side(d, carry):
        pl.semaphore_signal(barrier, inc=1, device_id=serve_peer(d)[3], device_id_type=MESH)
        return carry

    lax.fori_loop(4, 8, greet_side, 0)
    for device in (other_core, cross_up, cross_down):
        pl.semaphore_signal(barrier, inc=1, device_id=device, device_id_type=MESH)

    @pl.when(swap == 1)
    def _():
        pl.semaphore_signal(barrier, inc=1, device_id=swap_peer, device_id_type=MESH)

    def load(src, dst, i):
        return pltpu.make_async_copy(src, dst, load_sem.at[i])

    loads = [load(k_hbm, kbuf, 0), load(v_hbm, vbuf, 1)]
    loads.append(
        load(res_hbm.at[:, pl.ds(pl.multiple_of(blk * 256, 256), 256)], resb, 2)
    )
    for b in range(8):
        loads.append(load(ow_hbm.at[:, pl.ds(b * 256, 256)], owb.at[b], 3 + b))
    for one in loads:
        one.start()
    rt[0, 0:8, :] = ids_ref[...].astype(F32)
    rt[0, 8:16, :] = gates_ref[...]
    lens_t[...] = jnp.broadcast_to(len_ref[...].astype(F32), (128, 128)).T

    row = jnp.broadcast_to(map_ref[...].astype(F32), (128, 128))
    col = row.T
    sub = lax.broadcasted_iota(jnp.int32, (128, 128), 0)
    lane = lax.broadcasted_iota(jnp.int32, (128, 128), 1)
    again = jnp.where((row == col) & (lane < sub), 1.0, 0.0)
    eprim[...] = jnp.where(jnp.max(again, axis=1, keepdims=True) > 0.0, -1.0, col)

    loads[0].wait()
    loads[1].wait()
    scale = 128 ** (-0.5)
    rows_at = lax.broadcasted_iota(jnp.int32, (64, 1024), 0)
    cols_at = lax.broadcasted_iota(jnp.int32, (64, 1024), 1)
    same = (rows_at & 15) == (cols_at >> 6)
    at = (cols_at & 63).astype(F32)
    for g in range(4):
        lo = g * 16
        heads = [q_ref[lo : lo + 16, h * 128 : (h + 1) * 128] for h in range(4)]
        q16 = jnp.concatenate(heads, axis=0)
        k16 = kbuf[g * 1024 : (g + 1) * 1024, :]
        s = lax.dot_general(q16, k16, (((1,), (1,)), ((), ())), preferred_element_type=F32)
        own_len = lens_t[pl.ds(pl.multiple_of(xl * 64 + lo, 16), 16), :][:, 0:1]
        live = same & (at < jnp.concatenate([own_len] * 4, axis=0))
        s = jnp.where(live, s * scale, -1e30)
        peak = jnp.max(s, axis=1, keepdims=True)
        w = jnp.where(live, jnp.exp(s - peak), 0.0)
        total = jnp.sum(w, axis=1, keepdims=True)
        v16 = vbuf[g * 1024 : (g + 1) * 1024, :]
        a = jnp.dot(w.astype(BF16), v16, preferred_element_type=F32) / total
        a = a.astype(BF16)
        for h in range(4):
            att[h // 2, lo : lo + 16, (h % 2) * 128 : (h % 2 + 1) * 128] = a[
                h * 16 : (h + 1) * 16, :
            ]
    oh[xl] = att[xl]

    pl.semaphore_wait(barrier, 21 + swap)
    att_copy = remote(att.at[1 - xl], oh.at[xl], att_sems.at[0], att_sems.at[1], exp_peer)
    att_copy.start()

    weights = ((wg_hbm, wg), (wu_hbm, wu))

    def down_columns(k):
        return pl.ds(pl.multiple_of(lax.rem(y + k, 4) * 512, 512), 512)

    def swap_pieces(first, last):
        @pl.when(swap == 1)
        def _():
            for piece in range(first, last):
                if piece < 2:
                    i = piece
                    src, dst = weights[i][0], weights[i][1].at[1 - c]
                else:
                    k = BLOCKS[piece - 2]
                    i, src, dst = 2 + k, wd_hbm.at[:, down_columns(k)], wd.at[1 - c, k]
                remote(src, dst, w_send.at[i], w_in.at[i], swap_peer).start()


    def keep_weights():
        @pl.when(swap == 0)
        def _():
            for i, (src, dst) in enumerate(weights):
                pltpu.make_async_copy(src, dst.at[c], w_in.at[i]).start()
                remote(src, dst.at[c], w_send.at[i], w_other.at[i], other_core).start()
            for k in BLOCKS:
                src, dst = wd_hbm.at[:, down_columns(k)], wd.at[c, k]
                pltpu.make_async_copy(src, dst, w_in.at[2 + k]).start()
                remote(src, dst, w_send.at[2 + k], w_other.at[2 + k], other_core).start()

    for pos in range(1, NZ):
        remote(
            rt.at[0], rt.at[pos], rt_send.at[pos], rt_recv.at[pos], z_peer(NZ - ORDER[pos])
        ).start()

    for i in range(2, 11):
        loads[i].wait()
    att_copy.wait()
    heads_all = oh[...].reshape(128, 256)

    def scatter_copy(j, d):
        return remote(
            rs_send.at[j, d - 1],
            rs_recv.at[j, d - 1],
            rs_send_sem.at[j],
            rs_recv_sem.at[j],
            group_peer(d)[1],
        )

    def scatter(d, carry):
        part = jnp.dot(heads_all, owb[group_peer(d)[0]], preferred_element_type=F32)
        part = part.astype(BF16)
        rs_send[0, d - 1] = part[0:64, :]
        scatter_copy(0, d).start()
        rs_send[1, d - 1] = part[64:128, :]
        return carry

    def scatter_rest(d, carry):
        scatter_copy(1, d).start()
        return carry

    lax.fori_loop(1, 8, scatter, 0)
    lax.fori_loop(1, 8, scatter_rest, 0)
    own_out = jnp.dot(heads_all, owb[blk], preferred_element_type=F32)

    for pos in range(1, NZ):
        remote(
            rt.at[0], rt.at[pos], rt_send.at[pos], rt_recv.at[pos], z_peer(NZ - ORDER[pos])
        ).wait()
    first_slot = z * 16 + xh * 8 + xl * 4
    side_slot = z * 16 + (1 - xh) * 8 + (1 - xl) * 4
    expert = jnp.concatenate(
        [eprim[pl.ds(first_slot + i, 1), :] for i in range(4)]
        + [eprim[pl.ds(side_slot + i, 1), :] for i in range(4)],
        axis=0,
    )
    upper = jnp.where(sub < lane, 1.0, 0.0).astype(BF16)
    kk = lax.broadcasted_iota(jnp.int32, (2 * CAP, 256), 0).astype(F32)

    def routing(p, carry):
        places, probs = [], []
        for r in range(2):
            info = rt[2 * p + r]
            ids = info[0:8, :]
            gates = info[8:16, :]
            top = gates / jnp.sum(gates, axis=0, keepdims=True)
            named = jnp.zeros((8, 128), F32)
            prob = jnp.zeros((8, 128), F32)
            for j in range(8):
                hit = ids[j : j + 1, :] == expert
                named = jnp.where(hit, 1.0, named)
                prob = jnp.where(hit, top[j : j + 1, :], prob)
            before = jnp.dot(named.astype(BF16), upper, preferred_element_type=F32)
            places.append(jnp.where(named > 0.0, before + r * CAP, -100.0))
            probs.append(prob)
        place = jnp.concatenate(places, axis=1)
        prob = jnp.concatenate(probs, axis=1)
        for s in range(8):
            chosen = place[s : s + 1, :] == kk
            dmat[p, s] = jnp.where(chosen, 1.0, 0.0).astype(BF16)
            wmat[p, s] = jnp.where(chosen, prob[s : s + 1, :], 0.0).astype(BF16)
        return carry

    lax.fori_loop(0, PAIRS, routing, 0)

    def onward(pos_from, pos_to, step, j):
        return remote(
            xg.at[pos_from, j],
            xg.at[pos_to, j],
            xg_send.at[pos_to, j],
            xg_recv.at[pos_to, j],
            z_peer(step),
        )

    place_of = {offset: pos for pos, offset in enumerate(ORDER)}
    hops = {}
    for j in range(2):
        for k in range(4 - j):
            hops[place_of[k + 1], j] = onward(place_of[k], place_of[k + 1], NZ - 1, j)
        for k in range(3 + j):
            hops[place_of[NZ - 1 - k], j] = onward(
                place_of[(NZ - k) % NZ], place_of[NZ - 1 - k], 1, j
            )

    def share_squares(d, carry):
        remote(
            sq_send, sq_recv.at[d - 1], sq_sems.at[0], sq_sems.at[1], group_peer(d)[1]
        ).start()
        return carry

    def pair_copy(j):
        part = xg.at[0, j, xl]
        return remote(part, part, pair_send.at[j], pair_recv.at[j], exp_peer)

    gain = gain_ref[:, pl.ds(pl.multiple_of(blk * 256, 256), 256)]
    for j in range(2):
        pltpu.make_async_copy(rs_recv.at[j], rs_recv.at[j], rs_recv_sem.at[j]).wait()
        tokens = slice(64 * j, 64 * j + 64)
        total = resb[tokens, :].astype(F32) + own_out[tokens, :]
        for d in range(7):
            total = total + rs_recv[j, d].astype(F32)
        mixed[tokens, :] = total
        xg[0, j, xl] = (total * gain).astype(BF16)
        pair_copy(j).start()
        if j:
            total = mixed[...]
            sq_send[...] = lax.dot_general(
                jnp.ones((8, 256), F32),
                total * total,
                (((1,), (1,)), ((), ())),
                preferred_element_type=F32,
                precision=lax.Precision.HIGHEST,
            )
            lax.fori_loop(1, 8, share_squares, 0)
            swap_pieces(0, 6)
            keep_weights()
    for j in range(2):
        pair_copy(j).wait_recv()
        hops[1, j].start()
        hops[2, j].start()
    pltpu.make_async_copy(sq_recv, sq_recv, sq_sems.at[1]).wait()
    squares = sq_send[...]
    for d in range(7):
        squares = squares + sq_recv[d]
    sc[0] = lax.rsqrt(squares * (1.0 / 2048.0) + 1e-6)

    def scale_copy(pos):
        return remote(
            sc.at[0], sc.at[pos], sc_send.at[pos], sc_recv.at[pos], z_peer(NZ - ORDER[pos])
        )

    for pos in range(1, NZ):
        scale_copy(pos).start()

    forwards = {
        (1, 0): 3, (2, 0): 4, (1, 1): 3, (2, 1): 4, (3, 0): 5, (4, 0): 6,
        (3, 1): 5, (4, 1): 6, (5, 0): 7, (6, 1): 7,
    }
    for p in range(PAIRS):
        arrive = [pos for pos in (2 * p + 1, 2 * p + 2) if pos < NZ]
        for j in range(2):
            for pos in arrive:
                hops[pos, j].wait_recv()
                if (pos, j) in forwards:
                    hops[forwards[pos, j], j].start()
        scaled = []
        for pos in (2 * p, 2 * p + 1):
            if pos:
                scale_copy(pos).wait_recv()
            factor = jnp.broadcast_to(sc[pos, 0:1, :], (128, 128)).T
            factor = jnp.concatenate([factor, factor], axis=1)
            scaled.append(
                [
                    (xg[pos, :, h].reshape(128, 256).astype(F32) * factor).astype(BF16)
                    for h in range(2)
                ]
            )
        for half in range(2):
            rows = jnp.concatenate([scaled[0][half], scaled[1][half]], axis=0)
            picked = jnp.dot(dmat[p].reshape(384, 256), rows, preferred_element_type=F32)
            send1[p, :, :, half * 256 : (half + 1) * 256] = picked.astype(BF16).reshape(
                8, 2 * CAP, 256
            )

        def dispatch(d, carry, p=p):
            side, _, y_to, device = serve_peer(d)
            remote(
                send1.at[p, side * 4 + y_to],
                recv1.at[p, y, xh],
                a2a_send.at[p],
                a2a_recv.at[p],
                device,
            ).start()
            return carry

        lax.fori_loop(1, 8, dispatch, 0)
        pltpu.make_async_copy(send1.at[p, y], recv1.at[p, y, xh], a2a_recv.at[p]).start()

    def share(i, mine, other):
        pltpu.make_async_copy(mine, mine, w_in.at[i]).wait()

        @pl.when(swap == 1)
        def _():
            remote(mine, mine, fwd_send.at[i], w_other.at[i], other_core).start()

        return pltpu.make_async_copy(other, other, w_other.at[i])

    for one in [share(i, dst.at[c], dst.at[1 - c]) for i, (_, dst) in enumerate(weights)]:
        one.wait()
    contract = (((1,), (1,)), ((), ()))

    def hidden(p):
        pltpu.make_async_copy(recv1.at[p], recv1.at[p], a2a_recv.at[p]).wait()
        rows = jnp.concatenate(
            [recv1[p, b].reshape(4 * CAP, 512) for b in range(4)], axis=1
        )
        for half in range(2):
            gate = lax.dot_general(rows, wg[half], contract, preferred_element_type=F32)
            up = lax.dot_general(rows, wu[half], contract, preferred_element_type=F32)
            act[p, half] = (gate / (1.0 + jnp.exp(-gate)) * up).astype(BF16)

    def down_block(p, k):
        out = jnp.dot(act[p, 0], wd[0, k], preferred_element_type=F32)
        out = out + jnp.dot(act[p, 1], wd[1, k], preferred_element_type=F32)
        send2[p, k] = out.astype(BF16).reshape(2, 2 * CAP, 512)
        for d in (k, 4 + k):
            side, xh_to, _, device = serve_peer(d)
            src, dst = send2.at[p, k, xh_to], recv2.at[p, side * 4 + y]
            if d == 0:
                pltpu.make_async_copy(src, dst, back_recv.at[p]).start()
            else:
                remote(src, dst, back_send.at[p], back_recv.at[p], device).start()

    hidden(0)
    hidden(1)
    hidden(2)
    for k in BLOCKS:
        share(2 + k, wd.at[c, k], wd.at[1 - c, k]).wait()
        down_block(2, k)
    hidden(3)
    for p in (3, 1, 0):
        for k in BLOCKS:
            down_block(p, k)

    def xs_copy(p):
        return remote(
            xs_send.at[p], xs_recv.at[p], xs_send_sem.at[p], xs_recv_sem.at[p], exp_peer
        )

    def combine(p):
        pltpu.make_async_copy(recv2.at[p], recv2.at[p], back_recv.at[p]).wait()
        part = lax.dot_general(
            wmat[p].reshape(384, 256),
            recv2[p].reshape(384, 512),
            (((0,), (0,)), ((), ())),
            preferred_element_type=F32,
        )
        first, second = part[:, 0:256], part[:, 256:512]
        own_part[p] = jnp.where(xl == 0, first, second).reshape(2, 128, 256)
        xs_send[p] = jnp.where(xl == 0, second, first).astype(BF16).reshape(2, 128, 256)

    sent_up = {1: 1, 2: NZ - 1, 3: 2, 4: NZ - 1, 5: 1, 6: NZ - 2, 7: 2}
    added = {2: (4, 6), 3: (5, 7)}

    def z_copy(pos):
        i = pos - 1
        return remote(
            zs_send.at[i],
            zs_recv.at[i],
            zs_send_sem.at[i],
            zs_recv_sem.at[i],
            z_peer(sent_up[pos]),
        )

    def pass_on(pos, cross):
        piece = own_part[pos // 2, pos % 2]
        if cross:
            piece = piece + xs_recv[pos // 2, pos % 2].astype(F32)
        for other in added.get(pos, ()):
            z_copy(other).wait_recv()
            piece = piece + zs_recv[other - 1].astype(F32)
        zs_send[pos - 1] = piece.astype(BF16)
        z_copy(pos).start()

    last_copy = remote(
        xs_send.at[0, 0], xs_recv.at[0, 0], xs_send_sem.at[0], xs_recv_sem.at[0], exp_peer
    )
    cross_copy = remote(xs_send.at[0, 1], zx_recv, zx_sems.at[0], zx_sems.at[1], cross_up)
    combine(2)
    xs_copy(2).start()
    combine(3)
    xs_copy(3).start()
    for p in (2, 3):
        xs_copy(p).wait_recv()
        pass_on(2 * p, True)
        pass_on(2 * p + 1, True)
    combine(1)
    xs_copy(1).start()
    combine(0)
    last_copy.start()
    pass_on(1, False)
    cross_copy.start()
    xs_copy(1).wait_recv()
    pass_on(3, True)
    pass_on(2, True)
    total = mixed[...] + own_part[0, 0]
    last_copy.wait_recv()
    total = total + xs_recv[0, 0].astype(F32)
    cross_copy.wait_recv()
    total = total + zx_recv[...].astype(F32)
    for pos in (1, 2, 3):
        z_copy(pos).wait_recv()
        total = total + zs_recv[pos - 1].astype(F32)
    out_ref[...] = total.astype(BF16)

    for j in range(2):
        pltpu.make_async_copy(rs_send.at[j], rs_send.at[j], rs_send_sem.at[j]).wait()
        pair_copy(j).wait_send()
    pltpu.make_async_copy(sq_recv, sq_recv, sq_sems.at[0]).wait()
    for pos in range(1, NZ):
        z_copy(pos).wait_send()
    last_copy.wait_send()
    cross_copy.wait_send()
    for pos in range(1, NZ):
        hops[pos, 0].wait_send()
        hops[pos, 1].wait_send()
        scale_copy(pos).wait_send()
    for p in range(PAIRS):
        if p:
            xs_copy(p).wait_send()
        sent = send1.at[p, pl.ds(0, 7)]
        pltpu.make_async_copy(sent, sent, a2a_send.at[p]).wait()
        sent = recv2.at[p, pl.ds(0, 7)]
        pltpu.make_async_copy(sent, sent, back_send.at[p]).wait()
    halves = [wg.at[c], wu.at[c]] + [wd.at[c, k] for k in range(4)]
    for i, half in enumerate(halves):
        pltpu.make_async_copy(half, half, w_send.at[i]).wait()

    @pl.when(swap == 1)
    def _():
        for i, half in enumerate(halves):
            pltpu.make_async_copy(half, half, fwd_send.at[i]).wait()


def shards(
    queries,
    keys,
    values,
    lengths,
    out_weight,
    residual,
    norm_gain,
    expert_ids,
    gate_weights,
    replica_map,
    w_gate,
    w_up,
    w_down,
):
    vmem = pl.BlockSpec(memory_space=pltpu.VMEM)
    hbm = pl.BlockSpec(memory_space=pl.ANY)
    dma = pltpu.SemaphoreType.DMA
    return pl.pallas_call(
        layer_kernel,
        out_shape=jax.ShapeDtypeStruct((128, 256), BF16),
        in_specs=[vmem] * 6 + [hbm] * 7,
        out_specs=vmem,
        scratch_shapes=[
            pltpu.VMEM((4096, 128), BF16),
            pltpu.VMEM((4096, 128), BF16),
            pltpu.VMEM((8, 256, 256), BF16),
            pltpu.VMEM((128, 256), BF16),
            pltpu.VMEM((128, 128), F32),
            pltpu.VMEM((128, 128), F32),
            pltpu.VMEM((2, 64, 256), BF16),
            pltpu.VMEM((2, 64, 256), BF16),
            pltpu.VMEM((2, 7, 64, 256), BF16),
            pltpu.VMEM((2, 7, 64, 256), BF16),
            pltpu.VMEM((128, 256), F32),
            pltpu.VMEM((8, 128), F32),
            pltpu.VMEM((7, 8, 128), F32),
            pltpu.VMEM((8, 8, 128), F32),
            pltpu.VMEM((8, 16, 128), F32),
            pltpu.VMEM((8, 2, 2, 64, 256), BF16),
            pltpu.VMEM((PAIRS, 8, 2 * CAP, 256), BF16),
            pltpu.VMEM((PAIRS, 8, 2 * CAP, 256), BF16),
            pltpu.VMEM((PAIRS, 8, 2 * CAP, 512), BF16),
            pltpu.VMEM((PAIRS, 4, 2, 2 * CAP, 512), BF16),
            pltpu.VMEM((PAIRS, 4, 2, 2 * CAP, 512), BF16),
            pltpu.VMEM((PAIRS, 8, 2 * CAP, 512), BF16),
            pltpu.VMEM((PAIRS, 2, 128, 256), F32),
            pltpu.VMEM((PAIRS, 2, 128, 256), BF16),
            pltpu.VMEM((PAIRS, 2, 128, 256), BF16),
            pltpu.VMEM((7, 128, 256), BF16),
            pltpu.VMEM((7, 128, 256), BF16),
            pltpu.VMEM((128, 256), BF16),
            pltpu.VMEM((2, 192, 2048), BF16),
            pltpu.VMEM((2, 192, 2048), BF16),
            pltpu.VMEM((2, 4, 192, 512), BF16),
            pltpu.VMEM((PAIRS, 2, 4 * CAP, 192), BF16),
            dma((11,)),
            dma((6,)),
            dma((6,)),
            dma((6,)),
            dma((6,)),
            dma((2,)),
            dma((2,)),
            dma((2,)),
            dma((2,)),
            dma((2,)),
            dma((2,)),
            dma((8,)),
            dma((8,)),
            dma((8,)),
            dma((8,)),
            dma((8, 2)),
            dma((8, 2)),
            dma((PAIRS,)),
            dma((PAIRS,)),
            dma((PAIRS,)),
            dma((PAIRS,)),
            dma((PAIRS,)),
            dma((PAIRS,)),
            dma((7,)),
            dma((7,)),
            dma((2,)),
        ],
        compiler_params=pltpu.CompilerParams(
            collective_id=0, has_side_effects=True, vmem_limit_bytes=56 * 2**20
        ),
        name="layer",
    )(
        queries,
        lengths.reshape(1, 128),
        norm_gain.reshape(1, 2048),
        expert_ids.T,
        gate_weights.T,
        replica_map.reshape(1, 128),
        keys.reshape(4096, 128),
        values.reshape(4096, 128),
        out_weight,
        residual,
        w_gate.reshape(2048, 192).T,
        w_up.reshape(2048, 192).T,
        w_down.reshape(192, 2048),
    )


def solution(mesh):
    in_specs = (
        P(("req", "exp"), "kvh"),
        P(("req", "exp"), "kvh", None, None),
        P(("req", "exp"), "kvh", None, None),
        P("req"),
        P(("kvh", "exp"), None),
        P("req", None),
        P(),
        P("req", None),
        P("req", None),
        P(),
        P(("req", "kvh"), None, "exp"),
        P(("req", "kvh"), None, "exp"),
        P(("req", "kvh"), "exp", None),
    )
    out_specs = P("req", ("kvh", "exp"))
    return jax.shard_map(shards, mesh=mesh, in_specs=in_specs, out_specs=out_specs, check_vma=False)
```
